256 devices in a mesh: slab: 8 (over x, core), patch: 32 (over z, y).
Axes of the slice: x: 4, y: 4, z: 8, core: 2. Of those that a mesh axis runs over, the one named last changes fastest.
Arguments:
- right_side: float32 [8, 32, 256, 768], P('slab', 'patch'), may hold values from -6 to 6
- inverse_factor: bfloat16 [8, 32, 768, 768], P('slab', 'patch'), may hold values from -0.12990381 to 1.5, as said below
- forward_trace: bfloat16 [8, 32, 128, 768], P('slab', 'patch'), may hold values from -0.375 to 0.375
- backward_trace: bfloat16 [8, 32, 128, 768], P('slab', 'patch'), may hold values from -0.375 to 0.375
- margin: int32 [8, 32], P('slab', 'patch'), may hold values from 1 to 256, as said below
Outputs:
- correction: float32 [8, 32, 256, 768], P('slab', 'patch')
The draws below stay inside these ranges and needn't reach their ends.
Inputs may be any that keep to these rules, and one draw needn't show every extreme that they name: `inverse_factor`: lower triangular: zero above the diagonal, positive on it. margin[s, q] counts the last unknowns of patch q that are the first unknowns of patch q + 1 (of patch 0 for q = 31). In every slab some pair shares exactly 256.
All inputs are finite; a program needn't handle non-finite values.
Results may differ from the reference program's by a relative error of at most 0.035.
Values may be sent and summed in bfloat16 or wider, within the bound.
No kernel may reach another device: no remote copies, remote signals or barrier semaphores. Data moves between devices by JAX's collectives and lax.ppermute only.
A program may use at most 64 MiB of HBM per device.

```python
import math
import jax
import jax.numpy as jnp
from jax import lax

M = 768
KMAX = 256
FACE = 128
COLS = 256
SLABS = 8
PATCHES = 32


def draw_inverse_factor(key, part):
    first_key = jax.random.fold_in(key, 11)
    second_key = jax.random.fold_in(key, 12)
    full_shape = (SLABS, PATCHES, M, M)
    spread = jnp.clip(0.6 * jax.random.normal(first_key, full_shape, jnp.float32), -3.6, 3.6)
    diagonal = jax.random.uniform(second_key, (SLABS, PATCHES, M), jnp.float32, 0.7, 1.3)
    row_index = jnp.arange(M)[:, None]
    col_index = jnp.arange(M)[None, :]
    lower_part = jnp.where(row_index > col_index, spread, 0.0) / math.sqrt(M)
    matrix = lower_part + jnp.where(row_index == col_index, 1.0, 0.0) * diagonal[..., :, None]
    return matrix.astype(jnp.bfloat16)


def draw_margin(key, part):
    values = jax.random.randint(jax.random.fold_in(key, 21), (SLABS, PATCHES), 1, KMAX + 1)
    chosen = jax.random.randint(jax.random.fold_in(key, 22), (SLABS, 1), 0, PATCHES)
    return jnp.where(jnp.arange(PATCHES)[None, :] == chosen, KMAX, values).astype(jnp.int32)


def steps_of(key, shape, cuts, least, largest):
    level, own = 1.0, jax.random.fold_in(key, 6)
    for axis_at, shards_of in cuts:
        draws = jnp.exp(jax.random.uniform(jax.random.fold_in(own, axis_at), (shards_of,), jnp.float32, least / len(cuts), largest / len(cuts)))
        level = level * jnp.repeat(draws, shape[axis_at] // shards_of).reshape([-1 if axis == axis_at else 1 for axis in range(len(shape))])
    return level


def gaussian(stream_key, extent, width, bound, cuts=(), kind=jnp.bfloat16):
    drawn = jax.random.normal(stream_key, extent, jnp.float32) * width
    if len(cuts) > 0:
        drawn = steps_of(stream_key, extent, cuts, -0.22, 0.18) * drawn
    return jnp.clip(drawn, min=-bound, max=bound).astype(kind)


def setup_inputs(seed: int = 0) -> dict:
    keys = jax.random.split(jax.random.key(seed), 6)
    right_side = gaussian(keys[0], (SLABS, PATCHES, COLS, M), 1.0, 6.0, ((0, 8), (1, 32)), jnp.float32)
    inverse_factor = draw_inverse_factor(jax.random.fold_in(keys[5], 71), 0)
    forward_trace = gaussian(keys[2], (SLABS, PATCHES, FACE, M), (2 * FACE) ** -0.5, 0.375, ((0, 8), (1, 32)))
    backward_trace = gaussian(keys[3], (SLABS, PATCHES, FACE, M), (2 * FACE) ** -0.5, 0.375, ((0, 8), (1, 32)))
    margin = draw_margin(jax.random.fold_in(keys[5], 71), 0)
    return {"right_side": right_side, "inverse_factor": inverse_factor, "forward_trace": forward_trace, "backward_trace": backward_trace, "margin": margin}


def to_half(values):
    return lax.optimization_barrier(values.astype(jnp.bfloat16)).astype(jnp.float32)


def placement(counts):
    source_index = jnp.arange(KMAX, dtype=jnp.int32)[None, :, None]
    target_index = jnp.arange(KMAX, dtype=jnp.int32)[None, None, :]
    limit = counts.astype(jnp.int32)[:, None, None]
    hit = (source_index == KMAX - limit + target_index) & (target_index < limit)
    return jnp.where(hit, 1.0, 0.0).astype(jnp.float32)


def solve(values, factor):
    halfway = to_half(jnp.einsum('pck,pik->pci', to_half(values), factor))
    return jnp.einsum('pci,pik->pck', halfway, factor)


def slab_step(residual, factor, counts):
    initial = to_half(solve(residual, factor))
    placing = placement(counts)
    tail_rows = initial[:, :, M - KMAX:]
    head_rows = initial[:, :, :KMAX]
    from_left = jnp.roll(jnp.einsum('pcs,psd->pcd', tail_rows, placing), 1, axis=0)
    from_right = jnp.einsum('pci,pti->pct', jnp.roll(head_rows, -1, axis=0), placing)
    middle = jnp.zeros((residual.shape[0], residual.shape[1], M - 2 * KMAX), jnp.float32)
    shared = jnp.concatenate([from_left, middle, from_right], axis=2)
    return solve(residual - 0.5 * shared, factor)


def face_map(matrix, corrected):
    return to_half(jnp.einsum('pck,ptk->pct', to_half(corrected), matrix))


def face_terms(down_face, up_face):
    middle = jnp.zeros((down_face.shape[0], down_face.shape[1], M - 2 * FACE), jnp.float32)
    return jnp.concatenate([down_face, middle, up_face], axis=2)


def reference(right_side, inverse_factor, forward_trace, backward_trace, margin):
    zero_face = jnp.zeros((PATCHES, COLS, FACE), jnp.float32)
    down_store = []
    arriving = zero_face
    forward_last = None
    for slab_index in range(SLABS):
        factor = inverse_factor[slab_index].astype(jnp.float32)
        residual = right_side[slab_index] - face_terms(arriving, zero_face)
        corrected = slab_step(residual, factor, margin[slab_index])
        down_store.append(arriving)
        arriving = face_map(forward_trace[slab_index].astype(jnp.float32), corrected)
        forward_last = corrected
    results = [None] * SLABS
    up_face = zero_face
    for slab_index in range(SLABS - 1, -1, -1):
        factor = inverse_factor[slab_index].astype(jnp.float32)
        if slab_index == SLABS - 1:
            corrected = forward_last
        else:
            residual = right_side[slab_index] - face_terms(down_store[slab_index], up_face)
            corrected = slab_step(residual, factor, margin[slab_index])
        results[slab_index] = corrected
        up_face = face_map(backward_trace[slab_index].astype(jnp.float32), corrected)
    return jnp.stack(results, axis=0)
```

```python
import jax
import jax.numpy as jnp
from jax import lax
from jax.sharding import PartitionSpec as P

M = 768
KMAX = 256
FACE = 128
BF = jnp.bfloat16
F32 = jnp.float32
AXES = ("slab", "patch")


def dot(a, b):
    return lax.dot_general(a, b, (((1,), (0,)), ((), ())), preferred_element_type=F32)


def dot_t(a, b):
    return lax.dot_general(a, b, (((1,), (1,)), ((), ())), preferred_element_type=F32)


def t_dot(a, b):
    return lax.dot_general(a, b, (((0,), (0,)), ((), ())), preferred_element_type=F32)


def placement(limit):
    source = lax.broadcasted_iota(jnp.int32, (KMAX, KMAX), 0)
    target = lax.broadcasted_iota(jnp.int32, (KMAX, KMAX), 1)
    hit = (source == KMAX - limit + target) & (target < limit)
    return jnp.where(hit, 1.0, 0.0).astype(BF)


def prepare(residual, factor, down_map, up_map, limit):
    rows = jnp.concatenate([residual.astype(BF), down_map, up_map], axis=0)
    solved = dot(dot_t(rows, factor).astype(BF), factor).astype(BF)
    low = t_dot(factor[:, :FACE], factor)
    high = t_dot(factor[M - FACE :, M - FACE :], factor[M - FACE :])
    basis = jnp.concatenate([low, high], axis=0).astype(BF)
    columns = residual.shape[0]
    both = jnp.concatenate([solved[:columns], basis], axis=0)
    tail = dot(both[:, M - KMAX :], placement(limit)).astype(BF)
    return tail, both[:, :KMAX], solved[columns:]


def local_operators(residual, left, right, maps, limit):
    columns = residual.shape[0]
    right = dot_t(right, placement(limit)).astype(BF)
    middle = jnp.zeros((columns, M - 2 * KMAX), F32)
    shared = jnp.concatenate([left[:columns].astype(F32), middle, right[:columns].astype(F32)], axis=1)
    adjusted = residual - 0.5 * shared
    terms = dot_t(adjusted.astype(BF), maps)
    from_left = (0.5 * dot_t(left[columns:], maps[:, :KMAX])).astype(BF)
    from_right = (0.5 * dot_t(right[columns:], maps[:, M - KMAX :])).astype(BF)

    def stack(inputs, outputs, own):
        return jnp.concatenate([from_left[inputs, outputs], -own.T, from_right[inputs, outputs]], axis=0)

    down, up = slice(0, FACE), slice(FACE, 2 * FACE)
    down_down = stack(down, down, maps[:FACE, :FACE])
    down_up = stack(down, up, maps[FACE:, :FACE])
    up_up = stack(up, up, maps[FACE:, M - FACE :])
    return adjusted, right, terms[:, :FACE], terms[:, FACE:], down_down, down_up, up_up


def finish(adjusted, left, right, down, up, factor):
    columns = adjusted.shape[0]

    def side(at, basis):
        part = slice(at * FACE, (at + 1) * FACE)
        return 0.5 * dot(jnp.concatenate([down[:, part], up[:, part]], axis=1), basis)

    own = slice(FACE, 2 * FACE)
    low = side(0, left[columns:])
    high = side(2, right[columns:])
    low = low - jnp.pad(down[:, own].astype(F32), ((0, 0), (0, KMAX - FACE)))
    high = high - jnp.pad(up[:, own].astype(F32), ((0, 0), (KMAX - FACE, 0)))
    middle = jnp.zeros((columns, M - 2 * KMAX), F32)
    adjusted = adjusted + jnp.concatenate([low, middle, high], axis=1)
    return dot(dot_t(adjusted.astype(BF), factor).astype(BF), factor)


def on_device(right_side, inverse_factor, forward_trace, backward_trace, margin):
    slabs = lax.axis_size("slab")
    patches = lax.axis_size("patch")
    chips = slabs // 2

    def place(slab, patch):
        return slab * patches + patch % patches

    everywhere = [(slab, patch) for slab in range(slabs) for patch in range(patches)]

    def send(value, pairs):
        return lax.ppermute(value, AXES, pairs)

    def swap(value):
        return send(value, [(place(s, q), place(s ^ 1, q)) for s, q in everywhere])

    def neighbours(to_next, to_previous):
        left = send(to_next, [(place(s, q), place(s, q + 1)) for s, q in everywhere])
        right = send(to_previous, [(place(s, q), place(s, q - 1)) for s, q in everywhere])
        return left, right

    def hop(value, chip, step):
        even, odd, shift = 2 * chip, 2 * chip + 1, 2 * step
        found = []
        for by in (2, 1):
            pairs = [(place(even, q), place(even + shift, q + by)) for q in range(patches)]
            pairs += [(place(odd, q), place(odd + shift, q - by)) for q in range(patches)]
            found.append(send(value, pairs))
        found.append(send(value, [(place(even, q), place(even + shift, q)) for q in range(patches)]))
        return jnp.concatenate(found, axis=1)

    first = lax.axis_index("slab") % 2 == 0

    def pick(on_first, on_second):
        return jnp.where(first, on_first, on_second)

    residual = right_side[0, 0]
    factor = inverse_factor[0, 0]
    limit = margin[0, 0]
    columns = residual.shape[0]

    def block(array, at):
        return array[at * FACE : (at + 1) * FACE]

    tail, head, maps = prepare(residual, factor, forward_trace[0, 0], backward_trace[0, 0], limit)
    left, right = neighbours(tail, head)
    adjusted, right, down0, up0, down_down, down_up, up_up = local_operators(
        residual, left, right, maps, limit
    )
    down0_half = down0.astype(BF)
    inner = pick(down_down, up_up)
    outer = pick(up_up, down_down)
    message = jnp.concatenate([down0_half, inner], axis=0)
    got_left, got_right = neighbours(message, message)
    swapped = swap(jnp.concatenate([down0_half, outer], axis=0))
    outer = swapped[columns:]
    inner3 = [got_left[columns:], inner, got_right[columns:]]
    down3 = jnp.concatenate([got_left[:columns], down0_half, got_right[:columns]], axis=1)
    products = [dot(inner3[m], block(outer, m)) for m in range(3)]
    pair = [sum(block(products[m], at - m) for m in range(3) if 0 <= at - m < 3) for at in range(5)]
    start = swapped[:columns].astype(F32) + dot(down3, outer)
    low_blocks = jnp.concatenate([pair[0], pair[1], pair[2]], axis=0).astype(BF)
    high_blocks = jnp.concatenate([pair[4], pair[3], pair[2]], axis=0).astype(BF)
    kept = pick(low_blocks, high_blocks)
    got = swap(pick(high_blocks, low_blocks))
    forward_pair = pick(kept, got)
    backward_pair = pick(got, kept)

    def sweep(base, operator, order, step):
        arrived = jnp.zeros((columns, 3 * FACE), BF)
        for position, chip in enumerate(order):
            part = base if position == 0 else base + dot(arrived, operator)
            total = (part + swap(part)).astype(BF)
            arrived = arrived + hop(total, chip, step)
        other = swap(arrived)
        low, high = pick(arrived, other), pick(other, arrived)
        return jnp.concatenate([low, high[:, FACE : 2 * FACE], high[:, :FACE]], axis=1)

    def between(base3, faces5):
        found = []
        for m in range(3):
            part = slice(m * FACE, (m + 1) * FACE)
            reach = slice(m * FACE, (m + 3) * FACE)
            found.append(base3[:, part].astype(F32) + dot(faces5[:, reach], inner3[m]))
        return jnp.concatenate(found, axis=1).astype(BF)

    middle3 = slice(FACE, 4 * FACE)
    base = pick(start, jnp.zeros_like(start))
    down5 = sweep(base, forward_pair, range(chips - 1), 1)
    down = pick(down5[:, middle3], swap(between(down3, down5)))
    up0 = up0 + dot(down, down_up)
    up0_half = up0.astype(BF)
    up_left, up_right = neighbours(up0_half, up0_half)
    up3 = jnp.concatenate([up_left, up0_half, up_right], axis=1)
    base = pick(up0, dot(up3, outer))
    up5 = sweep(base, backward_pair, range(chips - 1, 0, -1), -1)
    up = pick(swap(between(up3, up5)), up5[:, middle3])
    return finish(adjusted, left, right, down, up, factor)[None, None]


def solution(mesh):
    placed = (
        P("slab", "patch", None, None),
        P("slab", "patch", None, None),
        P("slab", "patch", None, None),
        P("slab", "patch", None, None),
        P("slab", "patch"),
    )
    return jax.shard_map(
        on_device,
        mesh=mesh,
        in_specs=placed,
        out_specs=P("slab", "patch", None, None),
        check_vma=False,
    )
```

```python
import jax
import jax.numpy as jnp
from jax import lax
from jax.experimental import pallas as pl
from jax.experimental.pallas import tpu as pltpu
from jax.sharding import PartitionSpec as P

M = 768
KMAX = 256
FACE = 128
BF = jnp.bfloat16
F32 = jnp.float32
AXES = ("slab", "patch")
VMEM = pl.BlockSpec(memory_space=pltpu.VMEM)
SMEM = pl.BlockSpec(memory_space=pltpu.SMEM)


def dot(a, b):
    return lax.dot_general(a, b, (((1,), (0,)), ((), ())), preferred_element_type=F32)


def dot_t(a, b):
    return lax.dot_general(a, b, (((1,), (1,)), ((), ())), preferred_element_type=F32)


def placement(limit):
    source = lax.broadcasted_iota(jnp.int32, (KMAX, KMAX), 0)
    target = lax.broadcasted_iota(jnp.int32, (KMAX, KMAX), 1)
    hit = (source == KMAX - limit + target) & (target < limit)
    return jnp.where(hit, 1.0, 0.0).astype(BF)


def halves(rows, factor):
    found = []
    for at in range(0, M, KMAX):
        end = at + KMAX
        found.append(dot_t(rows[:, :end], factor[at:end, :end]).astype(BF))
    return jnp.concatenate(found, axis=1)


def call(kernel, shapes, scalars, arrays, cost):
    return pl.pallas_call(
        kernel,
        out_shape=[jax.ShapeDtypeStruct(shape, kind) for shape, kind in shapes],
        in_specs=[SMEM] + [VMEM] * len(arrays),
        out_specs=[VMEM] * len(shapes),
        cost_estimate=pl.CostEstimate(flops=cost[0], bytes_accessed=cost[1], transcendentals=0),
        compiler_params=pltpu.CompilerParams(vmem_limit_bytes=40 << 20),
    )(scalars, *arrays)


def prepare_kernel(scalars, residual, factor_ref, down_map, up_map, tail, head, maps):
    factor = factor_ref[...]
    columns = residual.shape[0]
    rows = jnp.concatenate([residual[...].astype(BF), down_map[...], up_map[...]], axis=0)
    half = halves(rows, factor)
    last = M - KMAX
    first_block = dot(half, factor[:, :KMAX]).astype(BF)
    last_block = dot(half[:, last:], factor[last:, last:]).astype(BF)
    middle_block = dot(half[columns:, KMAX:], factor[KMAX:, KMAX:last]).astype(BF)
    low = factor[:, :FACE].T
    high = factor[M - FACE :, M - FACE :].T
    head[:columns] = first_block[:columns]
    head[columns : columns + FACE] = dot(low, factor[:, :KMAX]).astype(BF)
    head[columns + FACE :] = dot(high, factor[M - FACE :, :KMAX]).astype(BF)
    ends = jnp.concatenate(
        [
            last_block[:columns],
            dot(low[:, last:], factor[last:, last:]).astype(BF),
            dot(high, factor[M - FACE :, last:]).astype(BF),
        ],
        axis=0,
    )
    tail[...] = dot(ends, placement(scalars[1])).astype(BF)
    maps[:, :KMAX] = first_block[columns:]
    maps[:, KMAX:last] = middle_block
    maps[:, last:] = last_block[columns:]


def prepare(scalars, residual, factor, down_map, up_map):
    columns = residual.shape[0]
    reach = columns + 2 * FACE
    shapes = [((reach, KMAX), BF), ((reach, KMAX), BF), ((2 * FACE, M), BF)]
    return call(prepare_kernel, shapes, scalars, [residual, factor, down_map, up_map], (1 << 30, 3 << 20))


def operators_kernel(
    scalars, residual, left, right, maps_ref, adjusted, right_basis, message, outer, extra, up_out
):
    columns = residual.shape[0]
    maps = maps_ref[...]
    first = scalars[0] == 0
    placed = dot_t(right[...], placement(scalars[1])).astype(BF)
    right_basis[...] = placed[columns:]
    adjusted[...] = residual[...]
    adjusted[:, :KMAX] = residual[:, :KMAX] - 0.5 * left[:columns].astype(F32)
    adjusted[:, M - KMAX :] = residual[:, M - KMAX :] - 0.5 * placed[:columns].astype(F32)
    terms = dot_t(adjusted[...].astype(BF), maps)
    from_left = (0.5 * dot_t(left[columns:], maps[:, :KMAX])).astype(BF)
    from_right = (0.5 * dot_t(placed[columns:], maps[:, M - KMAX :])).astype(BF)

    def stack(inputs, outputs, own):
        turned = (-own.astype(F32)).T.astype(BF)
        return jnp.concatenate([from_left[inputs, outputs], turned, from_right[inputs, outputs]], axis=0)

    down, up = slice(0, FACE), slice(FACE, 2 * FACE)
    down_down = stack(down, down, maps[:FACE, :FACE])
    down_up = stack(down, up, maps[FACE:, :FACE])
    up_up = stack(up, up, maps[FACE:, M - FACE :])
    down0 = terms[:, :FACE].astype(BF)
    message[:columns] = down0
    message[columns:] = jnp.where(first, down_down, up_up)
    outer[:columns] = down0
    outer[columns:] = jnp.where(first, up_up, down_down)
    extra[:columns] = terms[:, FACE:].astype(BF)
    extra[columns:] = down_up
    up_out[...] = terms[:, FACE:]


def local_operators(scalars, residual, left, right, maps):
    columns = residual.shape[0]
    pack = ((columns + 3 * FACE, FACE), BF)
    shapes = [((columns, M), F32), ((2 * FACE, KMAX), BF), pack, pack, pack, ((columns, FACE), F32)]
    return call(operators_kernel, shapes, scalars, [residual, left, right, maps], (1 << 28, 3 << 20))


def five(first, mine, other):
    low, high = jnp.where(first, mine, other), jnp.where(first, other, mine)
    return jnp.concatenate([low, high[:, FACE : 2 * FACE], high[:, :FACE]], axis=1)


def between(base3, faces5, rows3):
    found = []
    for m in range(3):
        part = slice(m * FACE, (m + 1) * FACE)
        reach = slice(m * FACE, (m + 3) * FACE)
        found.append((base3[:, part].astype(F32) + dot(faces5[:, reach], rows3[m])).astype(BF))
    return jnp.concatenate(found, axis=1)


def finish_kernel(
    scalars, adjusted, left_basis, right_basis, down, mine, other, up3, rows_l, rows_o, rows_r, factor_ref, out
):
    first = scalars[0] == 0
    factor = factor_ref[...]
    faces5 = five(first, mine[...], other[...])
    inside = between(up3[...], faces5, [rows_l[...], rows_o[...], rows_r[...]])
    up = jnp.where(first, inside, faces5[:, FACE : 4 * FACE])

    def side(at, basis):
        part = slice(at * FACE, (at + 1) * FACE)
        return 0.5 * dot(jnp.concatenate([down[:, part], up[:, part]], axis=1), basis)

    own = slice(FACE, 2 * FACE)
    low = adjusted[:, :KMAX] + side(0, left_basis[...])
    high = adjusted[:, M - KMAX :] + side(2, right_basis[...])
    rows = jnp.concatenate(
        [
            (low[:, :FACE] - down[:, own].astype(F32)).astype(BF),
            low[:, FACE:].astype(BF),
            adjusted[:, KMAX : M - KMAX].astype(BF),
            high[:, : KMAX - FACE].astype(BF),
            (high[:, KMAX - FACE :] - up[:, own].astype(F32)).astype(BF),
        ],
        axis=1,
    )
    half = halves(rows, factor)
    for at in range(0, M, KMAX):
        out[:, at : at + KMAX] = dot(half[:, at:], factor[at:, at : at + KMAX])


def on_device(right_side, inverse_factor, forward_trace, backward_trace, margin):
    slabs = lax.axis_size("slab")
    patches = lax.axis_size("patch")
    chips = slabs // 2

    def place(slab, patch):
        return slab * patches + patch % patches

    everywhere = [(slab, patch) for slab in range(slabs) for patch in range(patches)]

    def send(value, pairs):
        return lax.ppermute(value, AXES, pairs)

    def swap(value):
        return send(value, [(place(s, q), place(s ^ 1, q)) for s, q in everywhere])

    def neighbours(to_next, to_previous):
        left = send(to_next, [(place(s, q), place(s, q + 1)) for s, q in everywhere])
        right = send(to_previous, [(place(s, q), place(s, q - 1)) for s, q in everywhere])
        return left, right

    def outward(value):
        return send(value, [(place(s, q), place(s, q + (1 if s % 2 == 0 else -1))) for s, q in everywhere])

    def hop(value, chip, step):
        even, odd, shift = 2 * chip, 2 * chip + 1, 2 * step
        found = []
        for by in (2, 1):
            pairs = [(place(even, q), place(even + shift, q + by)) for q in range(patches)]
            pairs += [(place(odd, q), place(odd + shift, q - by)) for q in range(patches)]
            found.append(send(value, pairs))
        found.append(send(value, [(place(even, q), place(even + shift, q)) for q in range(patches)]))
        return jnp.concatenate(found, axis=1)

    core = lax.axis_index("slab") % 2
    first = core == 0

    def pick(on_first, on_second):
        return jnp.where(first, on_first, on_second)

    residual = right_side[0, 0]
    factor = inverse_factor[0, 0]
    columns = residual.shape[0]
    scalars = jnp.stack([core.astype(jnp.int32), margin[0, 0]])

    def block(array, at):
        return array[at * FACE : (at + 1) * FACE]

    tail, head, maps = prepare(scalars, residual, factor, forward_trace[0, 0], backward_trace[0, 0])
    left, right = neighbours(tail, head)
    adjusted, right_basis, message, outer, extra, up0 = local_operators(scalars, residual, left, right, maps)
    from_left, from_right = neighbours(message, message)
    swapped = swap(outer)

    down3 = jnp.concatenate([from_left[:columns], message[:columns], from_right[:columns]], axis=1)
    start = swapped[:columns].astype(F32) + dot(down3, swapped[columns:])
    base = pick(start, jnp.zeros_like(start))
    total = (base + swap(base)).astype(BF)
    total, packs = lax.optimization_barrier((total, (from_left, message, from_right, extra)))

    arrived = hop(total, 0, 1)
    others = [swap(pack) for pack in packs]
    even3 = [pick(mine, other) for mine, other in zip(packs[:3], others[:3])]
    odd3 = [pick(other, mine) for mine, other in zip(packs[:3], others[:3])]
    odd_extra = pick(others[3], packs[3])
    down3 = jnp.concatenate([pack[:columns] for pack in even3], axis=1)
    down_rows = [pack[columns:] for pack in even3]
    up_rows = [pack[columns:] for pack in odd3]
    odd_down = pick(swapped[columns:], outer[columns:])
    even_up = pick(outer[columns:], swapped[columns:])

    def compose(rows3, last):
        products = [dot(rows3[m], block(last, m)) for m in range(3)]
        pair = [sum(block(products[m], at - m) for m in range(3) if 0 <= at - m < 3) for at in range(5)]
        return jnp.concatenate([pick(pair[0], pair[4]), pick(pair[1], pair[3]), pair[2]], axis=0).astype(BF)

    forward_pair = compose(down_rows, odd_down)
    backward_pair = compose(up_rows, even_up)

    def sweep(base, arrived, operator, order, step):
        for chip in order:
            part = base if arrived is None else base + dot(arrived, operator)
            total = (part + swap(part)).astype(BF)
            new = hop(total, chip, step)
            arrived = new if arrived is None else arrived + new
        return arrived

    arrived = sweep(base, arrived, forward_pair, range(1, chips - 1), 1)
    down5 = five(first, arrived, swap(arrived))
    inside = between(down3, down5, down_rows)
    outside = down5[:, FACE : 4 * FACE]
    down = pick(outside, inside)
    odd_up0 = (odd_extra[:columns].astype(F32) + dot(inside, odd_extra[columns:])).astype(BF)
    even_up0 = up0 + dot(outside, extra[columns:])
    beside = outward(odd_up0)
    pair = jnp.concatenate([beside, pick(odd_up0, jnp.zeros_like(odd_up0))], axis=1)
    turn = jnp.concatenate([pick(block(even_up, 0), block(even_up, 2)), block(even_up, 1)], axis=0)
    base = pick(even_up0, jnp.zeros_like(even_up0)) + dot(pair, turn)
    arrived = sweep(base, None, backward_pair, range(chips - 1, 0, -1), -1)
    beside_other = swap(beside)
    up3 = jnp.concatenate([pick(beside, beside_other), odd_up0, pick(beside_other, beside)], axis=1)
    out = call(
        finish_kernel,
        [((columns, M), F32)],
        scalars,
        [adjusted, left[columns:], right_basis, down, arrived, swap(arrived), up3, *up_rows, factor],
        (1 << 29, 4 << 20),
    )[0]
    return out[None, None]


def solution(mesh):
    placed = (
        P("slab", "patch", None, None),
        P("slab", "patch", None, None),
        P("slab", "patch", None, None),
        P("slab", "patch", None, None),
        P("slab", "patch"),
    )
    return jax.shard_map(
        on_device,
        mesh=mesh,
        in_specs=placed,
        out_specs=P("slab", "patch", None, None),
        check_vma=False,
    )
```

```python
import functools

import jax
import jax.numpy as jnp
from jax import lax
from jax.experimental import pallas as pl
from jax.experimental.pallas import tpu as pltpu
from jax.sharding import PartitionSpec as P

M = 768
KMAX = 256
FACE = 128
BF = jnp.bfloat16
F32 = jnp.float32
AXES = ("slab", "patch")
VMEM = pl.BlockSpec(memory_space=pltpu.VMEM)
SMEM = pl.BlockSpec(memory_space=pltpu.SMEM)


def dot(a, b):
    return lax.dot_general(a, b, (((1,), (0,)), ((), ())), preferred_element_type=F32)


def dot_t(a, b):
    return lax.dot_general(a, b, (((1,), (1,)), ((), ())), preferred_element_type=F32)


def placement(limit):
    source = lax.broadcasted_iota(jnp.int32, (KMAX, KMAX), 0)
    target = lax.broadcasted_iota(jnp.int32, (KMAX, KMAX), 1)
    hit = (source == KMAX - limit + target) & (target < limit)
    return jnp.where(hit, 1.0, 0.0).astype(BF)


def halves(rows, factor):
    found = []
    for at in range(0, M, KMAX):
        end = at + KMAX
        found.append(dot_t(rows[:, :end], factor[at:end, :end]).astype(BF))
    return jnp.concatenate(found, axis=1)


def call(kernel, shapes, scalars, arrays, cost, spaces=None, scratch=()):
    return pl.pallas_call(
        kernel,
        out_shape=[jax.ShapeDtypeStruct(shape, kind) for shape, kind in shapes],
        in_specs=[SMEM] + (spaces or [VMEM] * len(arrays)),
        out_specs=[VMEM] * len(shapes),
        scratch_shapes=list(scratch),
        cost_estimate=pl.CostEstimate(flops=cost[0], bytes_accessed=cost[1], transcendentals=0),
        compiler_params=pltpu.CompilerParams(vmem_limit_bytes=40 << 20),
    )(scalars, *arrays)


def prepare_kernel(
    scalars, residual_in, factor_in, down_in, up_in, near, far, maps, residual, factor, down_map, up_map, sems
):
    last = M - KMAX
    copies = [
        pltpu.make_async_copy(source, target, sems.at[at])
        for at, (source, target) in enumerate(
            [
                (residual_in, residual),
                (down_in, down_map),
                (up_in, up_map),
                (factor_in.at[:KMAX], factor.at[:KMAX]),
                (factor_in.at[KMAX:last], factor.at[KMAX:last]),
                (factor_in.at[last:], factor.at[last:]),
            ]
        )
    ]
    for copy in copies:
        copy.start()
    columns = residual.shape[0]
    first = scalars[0] == 0
    for copy in copies[:4]:
        copy.wait()
    rows = jnp.concatenate([residual[...].astype(BF), down_map[...], up_map[...]], axis=0)
    half0 = dot_t(rows[:, :KMAX], factor[:KMAX, :KMAX]).astype(BF)
    copies[4].wait()
    half1 = dot_t(rows[:, :last], factor[KMAX:last, :last]).astype(BF)
    copies[5].wait()
    half2 = dot_t(rows, factor[last:, :]).astype(BF)
    half = jnp.concatenate([half0, half1, half2], axis=1)
    first_block = dot(half, factor[:, :KMAX]).astype(BF)
    last_block = dot(half2, factor[last:, last:]).astype(BF)
    middle_block = dot(half[columns:, KMAX:], factor[KMAX:, KMAX:last]).astype(BF)
    low = factor[:, :FACE].T
    high = factor[M - FACE :, M - FACE :].T
    head = jnp.concatenate(
        [
            first_block[:columns],
            dot(low, factor[:, :KMAX]).astype(BF),
            dot(high, factor[M - FACE :, :KMAX]).astype(BF),
        ],
        axis=0,
    )
    ends = jnp.concatenate(
        [
            last_block[:columns],
            dot(low[:, last:], factor[last:, last:]).astype(BF),
            dot(high, factor[M - FACE :, last:]).astype(BF),
        ],
        axis=0,
    )
    tail = dot(ends, placement(scalars[1])).astype(BF)
    near[...] = jnp.where(first, tail, head)
    far[...] = jnp.where(first, head, tail)
    maps[:, :KMAX] = first_block[columns:]
    maps[:, KMAX:last] = middle_block
    maps[:, last:] = last_block[columns:]


def prepare(scalars, residual, factor, down_map, up_map):
    columns = residual.shape[0]
    reach = columns + 2 * FACE
    shapes = [((reach, KMAX), BF), ((reach, KMAX), BF), ((2 * FACE, M), BF)]
    arrays = [residual, factor, down_map, up_map]
    scratch = [pltpu.VMEM(array.shape, array.dtype) for array in arrays] + [pltpu.SemaphoreType.DMA((6,))]
    spaces = [pl.BlockSpec(memory_space=pltpu.HBM)] * 4
    arrays = [pltpu.with_memory_space_constraint(array, pltpu.HBM) for array in arrays]
    return call(prepare_kernel, shapes, scalars, arrays, (1 << 30, 3 << 20), spaces, scratch)


def operators_kernel(
    scalars, residual, near, far, maps_ref, adjusted, near_basis, far_basis, message, outer, extra, up_out
):
    columns = residual.shape[0]
    maps = maps_ref[...]
    first = scalars[0] == 0
    left = jnp.where(first, near[...], far[...])
    right = jnp.where(first, far[...], near[...])
    right = dot_t(right, placement(scalars[1])).astype(BF)
    near_basis[...] = jnp.where(first, left[columns:], right[columns:])
    far_basis[...] = jnp.where(first, right[columns:], left[columns:])
    adjusted[...] = residual[...]
    adjusted[:, :KMAX] = residual[:, :KMAX] - 0.5 * left[:columns].astype(F32)
    adjusted[:, M - KMAX :] = residual[:, M - KMAX :] - 0.5 * right[:columns].astype(F32)
    terms = dot_t(adjusted[...].astype(BF), maps)
    from_left = (0.5 * dot_t(left[columns:], maps[:, :KMAX])).astype(BF)
    from_right = (0.5 * dot_t(right[columns:], maps[:, M - KMAX :])).astype(BF)
    from_near = jnp.where(first, from_left, from_right)
    from_far = jnp.where(first, from_right, from_left)

    def stack(inputs, outputs, own):
        turned = (-own.astype(F32)).T.astype(BF)
        return jnp.concatenate([from_near[inputs, outputs], turned, from_far[inputs, outputs]], axis=0)

    down, up = slice(0, FACE), slice(FACE, 2 * FACE)
    down_down = stack(down, down, maps[:FACE, :FACE])
    down_up = stack(down, up, maps[FACE:, :FACE])
    up_up = stack(up, up, maps[FACE:, M - FACE :])
    down0 = terms[:, :FACE].astype(BF)
    message[:columns] = down0
    message[columns:] = jnp.where(first, down_down, up_up)
    outer[:columns] = down0
    outer[columns:] = jnp.where(first, up_up, down_down)
    extra[:columns] = terms[:, FACE:].astype(BF)
    extra[columns:] = down_up
    up_out[...] = terms[:, FACE:]


def local_operators(scalars, residual, near, far, maps):
    columns = residual.shape[0]
    pack, basis = ((columns + 3 * FACE, FACE), BF), ((2 * FACE, KMAX), BF)
    shapes = [((columns, M), F32), basis, basis, pack, pack, pack, ((columns, FACE), F32)]
    return call(operators_kernel, shapes, scalars, [residual, near, far, maps], (1 << 28, 3 << 20))


def block(array, at):
    return array[at * FACE : (at + 1) * FACE]


def turned(rows):
    return jnp.concatenate([block(rows, 2), block(rows, 1), block(rows, 0)], axis=0)


def compose(rows3, last, width):
    products = [dot(rows3[m], block(last, m)) for m in range(3)]
    return [sum(block(products[m], at - m) for m in range(3) if 0 <= at - m < width) for at in range(width + 2)]


def share_kernel(
    scalars, near, own, far, far_o, own_o, near_o, outer, outer_o, extra, extra_o, up0,
    forward, backward, reach, reach_start, even_rows, odd_rows, even_down, turn, even_start,
):
    columns = own.shape[0] - 3 * FACE
    first = scalars[0] == 0

    def split(mine, other):
        a, b = mine[columns:], turned(other[columns:])
        return jnp.where(first, a, b), jnp.where(first, b, a)

    pairs = [split(near, far_o), split(own, own_o), split(far, near_o)]
    even3, odd3 = [pair[0] for pair in pairs], [pair[1] for pair in pairs]
    even_up, odd_down = split(outer, outer_o)
    even_mixed, odd_mixed = split(extra, extra_o)
    down3 = [
        jnp.where(first, mine[:columns], other[:columns])
        for mine, other in ((near, far_o), (own, own_o), (far, near_o))
    ]
    down3 = jnp.concatenate(down3, axis=1)
    even_down[...] = down3
    for at in range(3):
        even_rows[at * 3 * FACE : (at + 1) * 3 * FACE] = even3[at]
        odd_rows[at * 3 * FACE : (at + 1) * 3 * FACE] = odd3[at]
    forward[...] = jnp.concatenate(compose(even3, odd_down, 3), axis=0).astype(BF)
    backward[...] = jnp.concatenate(compose(odd3, even_up, 3), axis=0).astype(BF)
    up_other = extra_o[:columns].astype(F32)
    odd_start = jnp.where(first, up_other, up0[...]) + dot(down3, odd_mixed)
    reach_start[...] = odd_start
    reach[:columns] = odd_start.astype(BF)
    reach[columns:] = jnp.concatenate(compose(even3, odd_mixed, 3), axis=0).astype(BF)
    turn[: 3 * FACE] = even_mixed
    turn[3 * FACE :] = even_up
    even_start[...] = jnp.where(first, up0[...], up_other)


def turn_kernel(scalars, near, own, far, turn, even_start, operator, start):
    columns = even_start.shape[0]
    last = turn[3 * FACE :]
    far_rows = jnp.concatenate([block(far[columns:], at) for at in range(4, -1, -1)], axis=0)
    wide = compose([near[columns:], own[columns:], far_rows], last, 5)
    mixed = [block(turn, at).astype(F32) for at in range(3)]
    wide = [wide[at] + mixed[at - 2] if 2 <= at < 5 else wide[at] for at in range(7)]
    operator[...] = jnp.concatenate(wide, axis=0).astype(BF)
    rows = jnp.concatenate([near[:columns], own[:columns], far[:columns]], axis=1)
    start[...] = jnp.where(scalars[0] == 0, even_start[...] + dot(rows, last), 0.0)


def five(mine, other):
    own = mine[:, 2 * FACE :] + other[:, 2 * FACE :]
    return jnp.concatenate([mine[:, : 2 * FACE], own, other[:, FACE : 2 * FACE], other[:, :FACE]], axis=1)


def step_kernel(width, scalars, base, operator, reach, seen, reached, *refs):
    pieces, (part, seen_out, reached_out) = refs[:width], refs[-3:]
    start = reach.shape[0] - 5 * FACE
    total = base[...]
    between_total = reached[...]
    for at in range(width):
        piece = pieces[at][...]
        total += dot(piece, block(operator, at))
        here = at - (width - 3)
        if here >= 0:
            where = slice(here * FACE, (here + 1) * FACE)
            seen_out[:, where] = seen[:, where] + piece
            between_total += dot(piece, reach[start + here * FACE : start + (here + 1) * FACE])
    part[...] = total
    reached_out[...] = between_total


def close_kernel(scalars, seen, near, own, turn, even_start, base):
    total = dot(seen[:, FACE : 2 * FACE], block(turn, 0)) + dot(seen[:, 2 * FACE :], block(turn, 1))
    total += dot(near[...], block(turn, 3))
    base[...] = total + jnp.where(scalars[0] == 0, even_start[...] + dot(own[...], block(turn, 4)), 0.0)


def between(base3, faces5, rows):
    found = []
    for m in range(3):
        part = slice(m * FACE, (m + 1) * FACE)
        reach = slice(m * FACE, (m + 3) * FACE)
        inside = rows[m * 3 * FACE : (m + 1) * 3 * FACE]
        found.append((base3[:, part].astype(F32) + dot(faces5[:, reach], inside)).astype(BF))
    return jnp.concatenate(found, axis=1)


def faces_kernel(scalars, mine, other, even_down, even_rows, down):
    faces = five(mine, other)
    inside = between(even_down[...], faces, even_rows[...])
    down[...] = jnp.where(scalars[0] == 0, faces[:, FACE : 4 * FACE], inside)


def finish_kernel(
    scalars, adjusted, near_basis, far_basis, down, mine, other, near, own, far, near_l, own_l, far_l,
    odd_rows, factor_ref, out,
):
    first = scalars[0] == 0
    factor = factor_ref[...]
    faces = five(mine, other)
    last = scalars[2] == 1
    up3 = [jnp.where(last, late[...], early[...]) for early, late in ((near, near_l), (own, own_l), (far, far_l))]
    inside = between(jnp.concatenate(up3, axis=1), faces, odd_rows[...])
    up = jnp.where(first, inside, faces[:, FACE : 4 * FACE])

    def side(at, basis):
        part = slice(at * FACE, (at + 1) * FACE)
        return 0.5 * dot(jnp.concatenate([down[:, part], up[:, part]], axis=1), basis[...])

    own = slice(FACE, 2 * FACE)
    near, far = side(0, near_basis), side(2, far_basis)
    low = adjusted[:, :KMAX] + jnp.where(first, near, far)
    high = adjusted[:, M - KMAX :] + jnp.where(first, far, near)
    rows = jnp.concatenate(
        [
            (low[:, :FACE] - down[:, own].astype(F32)).astype(BF),
            low[:, FACE:].astype(BF),
            adjusted[:, KMAX : M - KMAX].astype(BF),
            high[:, : KMAX - FACE].astype(BF),
            (high[:, KMAX - FACE :] - up[:, own].astype(F32)).astype(BF),
        ],
        axis=1,
    )
    half = halves(rows, factor)
    for at in range(0, M, KMAX):
        out[:, at : at + KMAX] = dot(half[:, at:], factor[at:, at : at + KMAX])


def on_device(right_side, inverse_factor, forward_trace, backward_trace, margin):
    slabs = lax.axis_size("slab")
    patches = lax.axis_size("patch")
    chips = slabs // 2

    def place(slab, patch):
        return slab * patches + patch % patches

    everywhere = [(slab, patch) for slab in range(slabs) for patch in range(patches)]

    def send(value, pairs):
        return lax.ppermute(value, AXES, pairs)

    def swap(value):
        return send(value, [(place(s, q), place(s ^ 1, q)) for s, q in everywhere])

    def from_near(value):
        return send(value, [(place(s, q), place(s, q + (-1) ** s)) for s, q in everywhere])

    def from_far(value):
        return send(value, [(place(s, q), place(s, q - (-1) ** s)) for s, q in everywhere])

    def hop(value, chip, step, width):
        shift = 2 * step
        arrived = []
        for by in range(width, -1, -1):
            pairs = []
            for slab in (2 * chip, 2 * chip + 1)[: 2 if by else 1]:
                pairs += [(place(slab, q), place(slab + shift, q + by * (-1) ** slab)) for q in range(patches)]
            arrived.append(send(value, pairs))
        return arrived

    core = lax.axis_index("slab") % 2
    first = core == 0
    last_chip = lax.axis_index("slab") // 2 == chips - 1
    residual = right_side[0, 0]
    factor = inverse_factor[0, 0]
    columns = residual.shape[0]
    scalars = jnp.stack([core.astype(jnp.int32), margin[0, 0], last_chip.astype(jnp.int32)])
    face = (columns, FACE)
    three, five_, seven = 3 * FACE, 5 * FACE, 7 * FACE

    to_near, to_far, maps = prepare(scalars, residual, factor, forward_trace[0, 0], backward_trace[0, 0])
    near, far = from_near(to_near), from_far(to_far)
    adjusted, near_basis, far_basis, message, outer, extra, up0 = local_operators(
        scalars, residual, near, far, maps
    )
    near, far = from_near(message), from_far(message)
    outer_other = swap(outer)

    def joined(part):
        return (part + swap(part)).astype(BF)

    nothing = jnp.zeros(face, F32)
    down3 = jnp.concatenate([near[:columns], message[:columns], far[:columns]], axis=1)
    start = outer_other[:columns].astype(F32) + dot(down3, turned(outer_other[columns:]))
    base = jnp.where(first, start, nothing)
    total = joined(base)
    pieces = hop(total, 0, 1, 2)

    near_other, own_other, far_other, extra_other = [swap(pack) for pack in (near, message, far, extra)]
    rows = ((3 * three, FACE), BF)
    band = ((five_, FACE), BF)
    forward, backward, reach, reach_start, even_rows, odd_rows, even_down, turn, even_start = call(
        share_kernel,
        [band, band, ((columns + five_, FACE), BF), (face, F32), rows, rows, ((columns, three), BF),
         ((2 * three, FACE), BF), (face, F32)],
        scalars,
        [near, message, far, far_other, own_other, near_other, outer, outer_other, extra, extra_other, up0],
        (1 << 28, 4 << 20),
    )

    def step(pieces, base, operator, seen, reached, later=()):
        width = len(pieces)
        arrays = [base, operator, reach, seen, reached, *pieces, *later]
        spaces = [VMEM] * (5 + width) + [pl.BlockSpec(memory_space=pl.ANY)] * len(later)
        shapes = [(face, F32), ((columns, three), BF), (face, F32)]
        return call(functools.partial(step_kernel, width), shapes, scalars, arrays, (1 << 26, 1 << 19), spaces)

    unseen = jnp.zeros((columns, three), BF)
    part, seen, reached = step(pieces, base, forward, unseen, nothing)
    pieces = hop(joined(part), 1, 1, 2)
    reach_near = from_near(reach)
    part, seen, reached = step(pieces, base, forward, seen, reached, [reach_near])
    pieces = hop(joined(part), 2, 1, 3)

    operator, even_turn = call(
        turn_kernel,
        [((seven, FACE), BF), (face, F32)],
        scalars,
        [reach_near, reach, swap(reach_near), turn, even_start],
        (1 << 28, 2 << 20),
    )
    reached_other = swap(reached)
    part, seen_all, reached_last = step(pieces, even_turn, operator, seen, nothing, [reached_other])
    pieces = hop(joined(part), 3, -1, 2)

    own = (reach_start + reached + reached_other).astype(BF)
    near = from_near(own)
    base = call(close_kernel, [(face, F32)], scalars, [seen, near, own, turn, even_start], (1 << 27, 1 << 20))[0]
    reached_other = swap(reached_last)
    seen_other = swap(seen_all)
    part, seen, _ = step(pieces, base, backward, unseen, nothing, [reached_other, seen_other])
    pieces = hop(joined(part), 2, -1, 2)

    own_last = (reach_start + reached_last + reached_other).astype(BF)
    near_last = from_near(own_last)
    far = swap(near)
    down = call(
        faces_kernel, [((columns, three), BF)], scalars, [seen_all, seen_other, even_down, even_rows], (1 << 27, 1 << 20)
    )[0]
    part, seen, _ = step(pieces, base, backward, seen, nothing, [near_last, far, down])
    pieces = hop(joined(part), 1, -1, 2)
    far_last = swap(near_last)
    seen = seen + jnp.concatenate(pieces, axis=1)
    out = call(
        finish_kernel,
        [((columns, M), F32)],
        scalars,
        [
            adjusted, near_basis, far_basis, down, seen, swap(seen), near, own, far,
            near_last, own_last, far_last, odd_rows, factor,
        ],
        (1 << 29, 4 << 20),
    )[0]
    return out[None, None]


def solution(mesh):
    placed = (
        P("slab", "patch", None, None),
        P("slab", "patch", None, None),
        P("slab", "patch", None, None),
        P("slab", "patch", None, None),
        P("slab", "patch"),
    )
    return jax.shard_map(
        on_device,
        mesh=mesh,
        in_specs=placed,
        out_specs=P("slab", "patch", None, None),
        check_vma=False,
    )
```

```python
import jax
import jax.numpy as jnp
from jax import lax
from jax.experimental import pallas as pl
from jax.experimental.pallas import tpu as pltpu
from jax.sharding import PartitionSpec as P

M = 768
KMAX = 256
FACE = 128
BF = jnp.bfloat16
F32 = jnp.float32
AXES = ("slab", "patch")
VMEM = pl.BlockSpec(memory_space=pltpu.VMEM)
SMEM = pl.BlockSpec(memory_space=pltpu.SMEM)


def dot(a, b):
    return lax.dot_general(a, b, (((1,), (0,)), ((), ())), preferred_element_type=F32)


def dot_t(a, b):
    return lax.dot_general(a, b, (((1,), (1,)), ((), ())), preferred_element_type=F32)


def placement(limit):
    source = lax.broadcasted_iota(jnp.int32, (KMAX, KMAX), 0)
    target = lax.broadcasted_iota(jnp.int32, (KMAX, KMAX), 1)
    hit = (source == KMAX - limit + target) & (target < limit)
    return jnp.where(hit, 1.0, 0.0).astype(BF)


def halves(rows, factor):
    found = []
    for at in range(0, M, KMAX):
        end = at + KMAX
        found.append(dot_t(rows[:, :end], factor[at:end, :end]).astype(BF))
    return jnp.concatenate(found, axis=1)


def call(kernel, shapes, scalars, arrays, cost, spaces=None, scratch=()):
    return pl.pallas_call(
        kernel,
        out_shape=[jax.ShapeDtypeStruct(shape, kind) for shape, kind in shapes],
        in_specs=[SMEM] + (spaces or [VMEM] * len(arrays)),
        out_specs=[VMEM] * len(shapes),
        scratch_shapes=list(scratch),
        cost_estimate=pl.CostEstimate(flops=cost[0], bytes_accessed=cost[1], transcendentals=0),
        compiler_params=pltpu.CompilerParams(vmem_limit_bytes=40 << 20),
    )(scalars, *arrays)


def prepare_kernel(
    scalars, residual_in, factor_in, down_in, up_in, near, far, maps, residual, factor, down_map, up_map, sems
):
    last = M - KMAX
    copies = [
        pltpu.make_async_copy(source, target, sems.at[at])
        for at, (source, target) in enumerate(
            [
                (residual_in, residual),
                (down_in, down_map),
                (up_in, up_map),
                (factor_in.at[:KMAX, :KMAX], factor.at[:KMAX, :KMAX]),
                (factor_in.at[KMAX:last, :last], factor.at[KMAX:last, :last]),
                (factor_in.at[last:], factor.at[last:]),
            ]
        )
    ]
    for copy in copies:
        copy.start()
    columns = residual.shape[0]
    first = scalars[0] == 0
    for copy in copies[:4]:
        copy.wait()
    rows = jnp.concatenate([residual[...].astype(BF), down_map[...], up_map[...]], axis=0)
    half0 = dot_t(rows[:, :KMAX], factor[:KMAX, :KMAX]).astype(BF)
    copies[4].wait()
    half1 = dot_t(rows[:, :last], factor[KMAX:last, :last]).astype(BF)
    copies[5].wait()
    half2 = dot_t(rows, factor[last:, :]).astype(BF)
    half = jnp.concatenate([half0, half1, half2], axis=1)
    first_block = dot(half, factor[:, :KMAX]).astype(BF)
    last_block = dot(half2, factor[last:, last:]).astype(BF)
    middle_block = dot(half[columns:, KMAX:], factor[KMAX:, KMAX:last]).astype(BF)
    low = factor[:, :FACE].T
    high = factor[M - FACE :, M - FACE :].T
    head = jnp.concatenate(
        [
            first_block[:columns],
            dot(low, factor[:, :KMAX]).astype(BF),
            dot(high, factor[M - FACE :, :KMAX]).astype(BF),
        ],
        axis=0,
    )
    ends = jnp.concatenate(
        [
            last_block[:columns],
            dot(low[:, last:], factor[last:, last:]).astype(BF),
            dot(high, factor[M - FACE :, last:]).astype(BF),
        ],
        axis=0,
    )
    tail = dot(ends, placement(scalars[1])).astype(BF)
    near[...] = jnp.where(first, tail, head)
    far[...] = jnp.where(first, head, tail)
    maps[:, :KMAX] = first_block[columns:]
    maps[:, KMAX:last] = middle_block
    maps[:, last:] = last_block[columns:]


def prepare(scalars, residual, factor, down_map, up_map):
    columns = residual.shape[0]
    reach = columns + 2 * FACE
    shapes = [((reach, KMAX), BF), ((reach, KMAX), BF), ((2 * FACE, M), BF)]
    arrays = [residual, factor, down_map, up_map]
    scratch = [pltpu.VMEM(array.shape, array.dtype) for array in arrays] + [pltpu.SemaphoreType.DMA((6,))]
    spaces = [pl.BlockSpec(memory_space=pltpu.HBM)] * 4
    arrays = [pltpu.with_memory_space_constraint(array, pltpu.HBM) for array in arrays]
    return call(prepare_kernel, shapes, scalars, arrays, (1 << 30, 3 << 20), spaces, scratch)


def operators_kernel(
    scalars, residual, near, far, maps_ref, adjusted, near_basis, far_basis, message, outer, extra, up_out
):
    columns = residual.shape[0]
    maps = maps_ref[...]
    first = scalars[0] == 0
    left = jnp.where(first, near[...], far[...])
    right = jnp.where(first, far[...], near[...])
    right = dot_t(right, placement(scalars[1])).astype(BF)
    near_basis[...] = jnp.where(first, left[columns:], right[columns:])
    far_basis[...] = jnp.where(first, right[columns:], left[columns:])
    adjusted[...] = residual[...]
    adjusted[:, :KMAX] = residual[:, :KMAX] - 0.5 * left[:columns].astype(F32)
    adjusted[:, M - KMAX :] = residual[:, M - KMAX :] - 0.5 * right[:columns].astype(F32)
    terms = dot_t(adjusted[...].astype(BF), maps)
    from_left = (0.5 * dot_t(left[columns:], maps[:, :KMAX])).astype(BF)
    from_right = (0.5 * dot_t(right[columns:], maps[:, M - KMAX :])).astype(BF)
    from_near = jnp.where(first, from_left, from_right)
    from_far = jnp.where(first, from_right, from_left)

    def stack(inputs, outputs, own):
        turned = (-own.astype(F32)).T.astype(BF)
        return jnp.concatenate([from_near[inputs, outputs], turned, from_far[inputs, outputs]], axis=0)

    down, up = slice(0, FACE), slice(FACE, 2 * FACE)
    down_down = stack(down, down, maps[:FACE, :FACE])
    down_up = stack(down, up, maps[FACE:, :FACE])
    up_up = stack(up, up, maps[FACE:, M - FACE :])
    down0 = terms[:, :FACE].astype(BF)
    message[:columns] = down0
    message[columns:] = jnp.where(first, down_down, up_up)
    outer[:columns] = down0
    outer[columns:] = jnp.where(first, up_up, down_down)
    extra[:columns] = terms[:, FACE:].astype(BF)
    extra[columns:] = down_up
    up_out[...] = terms[:, FACE:]


def local_operators(scalars, residual, near, far, maps):
    columns = residual.shape[0]
    pack, basis = ((columns + 3 * FACE, FACE), BF), ((2 * FACE, KMAX), BF)
    shapes = [((columns, M), F32), basis, basis, pack, pack, pack, ((columns, FACE), F32)]
    return call(operators_kernel, shapes, scalars, [residual, near, far, maps], (1 << 28, 3 << 20))


def block(array, at):
    return array[at * FACE : (at + 1) * FACE]


def turned(rows):
    return jnp.concatenate([block(rows, 2), block(rows, 1), block(rows, 0)], axis=0)


def compose(rows3, last, width):
    products = [dot(rows3[m], block(last, m)) for m in range(3)]
    return [sum(block(products[m], at - m) for m in range(3) if 0 <= at - m < width) for at in range(width + 2)]


def share_kernel(
    scalars, near, own, far, outer, outer_o, extra, extra_o, up0,
    forward, backward, reach, reach_start, even_rows, odd_rows, even_down, turn, even_start,
):
    columns = up0.shape[0]
    end = columns + 3 * FACE
    first = scalars[0] == 0

    def split(mine, other):
        a, b = mine[columns:], turned(other[columns:])
        return jnp.where(first, a, b), jnp.where(first, b, a)

    even3 = [near[columns:end], own[columns:end], turned(far[columns:end])]
    odd3 = [near[end:], own[end:], turned(far[end:])]
    even_up, odd_down = split(outer, outer_o)
    even_mixed, odd_mixed = split(extra, extra_o)
    down3 = jnp.concatenate([near[:columns], own[:columns], far[:columns]], axis=1)
    even_down[...] = down3
    for at in range(3):
        even_rows[at * 3 * FACE : (at + 1) * 3 * FACE] = even3[at]
        odd_rows[at * 3 * FACE : (at + 1) * 3 * FACE] = odd3[at]
    forward[...] = jnp.concatenate(compose(even3, odd_down, 3), axis=0).astype(BF)
    backward[...] = jnp.concatenate(compose(odd3, even_up, 3), axis=0).astype(BF)
    up_other = extra_o[:columns].astype(F32)
    odd_start = jnp.where(first, up_other, up0[...]) + dot(down3, odd_mixed)
    reach_start[...] = odd_start
    reach[:columns] = odd_start.astype(BF)
    reach[columns:] = jnp.concatenate(compose(even3, odd_mixed, 3), axis=0).astype(BF)
    turn[: 3 * FACE] = even_mixed
    turn[3 * FACE :] = even_up
    even_start[...] = jnp.where(first, up0[...], up_other)


def turn_kernel(scalars, near, own, far, turn, even_start, operator, start):
    columns = even_start.shape[0]
    last = turn[3 * FACE :]
    far_rows = jnp.concatenate([block(far[columns:], at) for at in range(4, -1, -1)], axis=0)
    wide = compose([near[columns:], own[columns:], far_rows], last, 5)
    mixed = [block(turn, at).astype(F32) for at in range(3)]
    wide = [wide[at] + mixed[at - 2] if 2 <= at < 5 else wide[at] for at in range(7)]
    operator[...] = jnp.concatenate(wide, axis=0).astype(BF)
    rows = jnp.concatenate([near[:columns], own[:columns], far[:columns]], axis=1)
    start[...] = jnp.where(scalars[0] == 0, even_start[...] + dot(rows, last), 0.0)


def five(mine, other):
    own = mine[:, 2 * FACE :] + other[:, 2 * FACE :]
    return jnp.concatenate([mine[:, : 2 * FACE], own, other[:, FACE : 2 * FACE], other[:, :FACE]], axis=1)


def between(base3, faces5, rows):
    found = []
    for m in range(3):
        part = slice(m * FACE, (m + 1) * FACE)
        reach = slice(m * FACE, (m + 3) * FACE)
        inside = rows[m * 3 * FACE : (m + 1) * 3 * FACE]
        found.append((base3[:, part].astype(F32) + dot(faces5[:, reach], inside)).astype(BF))
    return jnp.concatenate(found, axis=1)


def faces_kernel(scalars, mine, other, even_down, even_rows, down):
    faces = five(mine, other)
    inside = between(even_down[...], faces, even_rows[...])
    down[...] = jnp.where(scalars[0] == 0, faces[:, FACE : 4 * FACE], inside)


def finish_kernel(
    scalars, adjusted, near_basis, far_basis, down, mine, other, near, own, far, odd_rows, factor_ref, out
):
    first = scalars[0] == 0
    factor = factor_ref[...]
    faces = five(mine, other)
    up3 = jnp.concatenate([near[...], own[...], far[...]], axis=1)
    inside = between(up3, faces, odd_rows[...])
    up = jnp.where(first, inside, faces[:, FACE : 4 * FACE])

    def side(at, basis):
        part = slice(at * FACE, (at + 1) * FACE)
        return 0.5 * dot(jnp.concatenate([down[:, part], up[:, part]], axis=1), basis[...])

    own = slice(FACE, 2 * FACE)
    near, far = side(0, near_basis), side(2, far_basis)
    low = adjusted[:, :KMAX] + jnp.where(first, near, far)
    high = adjusted[:, M - KMAX :] + jnp.where(first, far, near)
    rows = jnp.concatenate(
        [
            (low[:, :FACE] - down[:, own].astype(F32)).astype(BF),
            low[:, FACE:].astype(BF),
            adjusted[:, KMAX : M - KMAX].astype(BF),
            high[:, : KMAX - FACE].astype(BF),
            (high[:, KMAX - FACE :] - up[:, own].astype(F32)).astype(BF),
        ],
        axis=1,
    )
    half = halves(rows, factor)
    for at in range(0, M, KMAX):
        out[:, at : at + KMAX] = dot(half[:, at:], factor[at:, at : at + KMAX])


def on_device(right_side, inverse_factor, forward_trace, backward_trace, margin):
    slabs = lax.axis_size("slab")
    patches = lax.axis_size("patch")
    chips = slabs // 2

    def place(slab, patch):
        return slab * patches + patch % patches

    everywhere = [(slab, patch) for slab in range(slabs) for patch in range(patches)]

    def send(value, pairs):
        return lax.ppermute(value, AXES, pairs)

    def swap(value):
        return send(value, [(place(s, q), place(s ^ 1, q)) for s, q in everywhere])

    def from_near(value):
        return send(value, [(place(s, q), place(s, q + (-1) ** s)) for s, q in everywhere])

    def from_far(value):
        return send(value, [(place(s, q), place(s, q - (-1) ** s)) for s, q in everywhere])

    def hop(value, chip, step, width):
        shift = 2 * step
        arrived = []
        for by in range(width, -1, -1):
            pairs = []
            for slab in (2 * chip, 2 * chip + 1)[: 2 if by else 1]:
                pairs += [(place(slab, q), place(slab + shift, q + by * (-1) ** slab)) for q in range(patches)]
            arrived.append(send(value, pairs))
        return arrived

    core = lax.axis_index("slab") % 2
    first = core == 0
    def pick(on_first, on_second):
        return jnp.where(first, on_first, on_second)

    last_chip = lax.axis_index("slab") // 2 == chips - 1
    residual = right_side[0, 0]
    factor = inverse_factor[0, 0]
    columns = residual.shape[0]
    scalars = jnp.stack([core.astype(jnp.int32), margin[0, 0], last_chip.astype(jnp.int32)])
    face = (columns, FACE)
    three, five_, seven = 3 * FACE, 5 * FACE, 7 * FACE

    to_near, to_far, maps = prepare(scalars, residual, factor, forward_trace[0, 0], backward_trace[0, 0])
    near, far = from_near(to_near), from_far(to_far)
    adjusted, near_basis, far_basis, message, outer, extra, up0 = local_operators(
        scalars, residual, near, far, maps
    )

    message_other = swap(message)
    outer_other = swap(outer)
    mine, other = message[columns:], turned(message_other[columns:])
    pack = jnp.concatenate(
        [pick(message[:columns], message_other[:columns]), pick(mine, other), pick(other, mine)], axis=0
    )
    near = from_near(pack)

    def joined(part):
        return (part + swap(part)).astype(BF)

    nothing = jnp.zeros(face, F32)
    odd_down = pick(turned(outer_other[columns:]), outer[columns:])
    own_down = pick(pack[:columns], jnp.zeros(face, BF))
    base = dot(jnp.concatenate([near[:columns], own_down], axis=1), odd_down[: 2 * FACE])
    base = base + pick(outer_other[:columns].astype(F32), nothing)
    pieces = hop(joined(base), 0, 1, 2)

    far, extra_other = swap(near), swap(extra)
    rows = ((3 * three, FACE), BF)
    band = ((five_, FACE), BF)
    forward, backward, reach, reach_start, even_rows, odd_rows, even_down, turn, even_start = call(
        share_kernel,
        [band, band, ((columns + five_, FACE), BF), (face, F32), rows, rows, ((columns, three), BF),
         ((2 * three, FACE), BF), (face, F32)],
        scalars,
        [near, pack, far, outer, outer_other, extra, extra_other, up0],
        (1 << 10, 1 << 10),
    )

    def step(pieces, base, operator, *later, beside=()):
        pieces, base, operator, later, beside = barrier((pieces, base, operator, later, list(beside)))
        rows = jnp.concatenate([*pieces, *beside], axis=1)
        part = base + dot(rows, operator[: rows.shape[1]])
        part, pieces, beside = barrier((part, pieces, beside))
        return joined(part), jnp.concatenate(pieces[-3:], axis=1), *later, *beside

    def inward(seen):
        return dot(seen, reach[columns : columns + three])

    barrier = lax.optimization_barrier
    total, seen = step(pieces, base, forward)
    pieces = hop(total, 1, 1, 2)
    reach_near = from_near(reach)
    total, new, reach_near, seen = step(pieces, base, forward, reach_near, seen)
    pieces = hop(total, 2, 1, 3)
    seen = seen + new
    reached = inward(seen)

    operator, even_turn = call(
        turn_kernel,
        [((seven, FACE), BF), (face, F32)],
        scalars,
        [reach_near, reach, swap(reach_near), turn, even_start],
        (1 << 10, 1 << 10),
    )
    reached_other = swap(reached)
    total, new, reached_other, operator = step(pieces, even_turn, operator, reached_other, operator)
    pieces = hop(total, 3, -1, 2)

    seen_all = seen + new
    reached_last = inward(new)
    last_other = swap(reached_last)
    reached_other, last_other = barrier((reached_other, last_other))
    own = (reach_start + reached + reached_other).astype(BF)
    near = from_near(own)
    own_part = jnp.concatenate([seen[:, FACE:], pick(own, jnp.zeros(face, BF))], axis=1)
    own_turn = jnp.concatenate([turn[: 2 * FACE], turn[4 * FACE : 5 * FACE]], axis=0)
    near_turn = turn[3 * FACE : 4 * FACE]
    base = pick(even_start, nothing) + dot(own_part, own_turn)
    turned_back = jnp.concatenate([backward[:three], near_turn], axis=0)
    total, seen, last_other, near = step(pieces, base, turned_back, last_other, beside=[near])
    pieces = hop(total, 2, -1, 2)
    base = base + dot(near, near_turn)

    own_last = (reach_start + reached_last + last_other).astype(BF)
    near_last = from_near(own_last)
    seen_other = swap(seen_all)
    down = call(
        faces_kernel, [((columns, three), BF)], scalars, [seen_all, seen_other, even_down, even_rows], (1 << 10, 1 << 10)
    )[0]
    total, new, near_last, down = step(pieces, base, backward, near_last, down)
    pieces = hop(total, 1, -1, 2)
    seen = seen + new
    near, own = jnp.where(last_chip, near_last, near), jnp.where(last_chip, own_last, own)
    pieces, seen, far = barrier((pieces, seen, swap(near)))
    seen = seen + jnp.concatenate(pieces, axis=1)
    out = call(
        finish_kernel,
        [((columns, M), F32)],
        scalars,
        [
            adjusted, near_basis, far_basis, down, seen, swap(seen), near, own, far, odd_rows, factor,
        ],
        (1 << 29, 4 << 20),
    )[0]
    return out[None, None]


def solution(mesh):
    placed = (
        P("slab", "patch", None, None),
        P("slab", "patch", None, None),
        P("slab", "patch", None, None),
        P("slab", "patch", None, None),
        P("slab", "patch"),
    )
    return jax.shard_map(
        on_device,
        mesh=mesh,
        in_specs=placed,
        out_specs=P("slab", "patch", None, None),
        check_vma=False,
    )
```

```python
import jax
import jax.numpy as jnp
from jax import lax
from jax.experimental import pallas as pl
from jax.experimental.pallas import tpu as pltpu
from jax.sharding import PartitionSpec as P

M = 768
KMAX = 256
FACE = 128
BF = jnp.bfloat16
F32 = jnp.float32
AXES = ("slab", "patch")
VMEM = pl.BlockSpec(memory_space=pltpu.VMEM)
SMEM = pl.BlockSpec(memory_space=pltpu.SMEM)


def dot(a, b):
    return lax.dot_general(a, b, (((1,), (0,)), ((), ())), preferred_element_type=F32)


def dot_t(a, b):
    return lax.dot_general(a, b, (((1,), (1,)), ((), ())), preferred_element_type=F32)


def placement(limit):
    source = lax.broadcasted_iota(jnp.int32, (KMAX, KMAX), 0)
    target = lax.broadcasted_iota(jnp.int32, (KMAX, KMAX), 1)
    hit = (source == KMAX - limit + target) & (target < limit)
    return jnp.where(hit, 1.0, 0.0).astype(BF)


def halves(rows, factor):
    found = []
    for at in range(0, M, KMAX):
        end = at + KMAX
        found.append(dot_t(rows[:, :end], factor[at:end, :end]).astype(BF))
    return jnp.concatenate(found, axis=1)


def call(kernel, shapes, scalars, arrays, cost, spaces=None, scratch=()):
    return pl.pallas_call(
        kernel,
        out_shape=[jax.ShapeDtypeStruct(shape, kind) for shape, kind in shapes],
        in_specs=[SMEM] + (spaces or [VMEM] * len(arrays)),
        out_specs=[VMEM] * len(shapes),
        scratch_shapes=list(scratch),
        cost_estimate=pl.CostEstimate(flops=cost[0], bytes_accessed=cost[1], transcendentals=0),
        compiler_params=pltpu.CompilerParams(vmem_limit_bytes=40 << 20),
    )(scalars, *arrays)


def prepare_kernel(
    scalars, residual_in, factor_in, down_in, up_in, near, far, maps, residual, factor, down_map, up_map, sems
):
    last = M - KMAX
    copies = [
        pltpu.make_async_copy(source, target, sems.at[at])
        for at, (source, target) in enumerate(
            [
                (residual_in, residual),
                (down_in, down_map),
                (up_in, up_map),
                (factor_in.at[:KMAX, :KMAX], factor.at[:KMAX, :KMAX]),
                (factor_in.at[KMAX:last, :last], factor.at[KMAX:last, :last]),
                (factor_in.at[last:], factor.at[last:]),
            ]
        )
    ]
    for copy in copies:
        copy.start()
    columns = residual.shape[0]
    first = scalars[0] == 0
    for copy in copies[:4]:
        copy.wait()
    rows = jnp.concatenate([residual[...].astype(BF), down_map[...], up_map[...]], axis=0)
    half0 = dot_t(rows[:, :KMAX], factor[:KMAX, :KMAX]).astype(BF)
    copies[4].wait()
    half1 = dot_t(rows[:, :last], factor[KMAX:last, :last]).astype(BF)
    copies[5].wait()
    half2 = dot_t(rows, factor[last:, :]).astype(BF)
    half = jnp.concatenate([half0, half1, half2], axis=1)
    first_block = dot(half, factor[:, :KMAX]).astype(BF)
    last_block = dot(half2, factor[last:, last:]).astype(BF)
    middle_block = dot(half[columns:, KMAX:], factor[KMAX:, KMAX:last]).astype(BF)
    low = factor[:, :FACE].T
    high = factor[M - FACE :, M - FACE :].T
    head = jnp.concatenate(
        [
            first_block[:columns],
            dot(low, factor[:, :KMAX]).astype(BF),
            dot(high, factor[M - FACE :, :KMAX]).astype(BF),
        ],
        axis=0,
    )
    ends = jnp.concatenate(
        [
            last_block[:columns],
            dot(low[:, last:], factor[last:, last:]).astype(BF),
            dot(high, factor[M - FACE :, last:]).astype(BF),
        ],
        axis=0,
    )
    tail = dot(ends, placement(scalars[1])).astype(BF)
    near[...] = jnp.where(first, tail, head)
    far[...] = jnp.where(first, head, tail)
    maps[:, :KMAX] = first_block[columns:]
    maps[:, KMAX:last] = middle_block
    maps[:, last:] = last_block[columns:]


def prepare(scalars, residual, factor, down_map, up_map):
    columns = residual.shape[0]
    reach = columns + 2 * FACE
    shapes = [((reach, KMAX), BF), ((reach, KMAX), BF), ((2 * FACE, M), BF)]
    arrays = [residual, factor, down_map, up_map]
    scratch = [pltpu.VMEM(array.shape, array.dtype) for array in arrays] + [pltpu.SemaphoreType.DMA((6,))]
    spaces = [pl.BlockSpec(memory_space=pltpu.HBM)] * 4
    arrays = [pltpu.with_memory_space_constraint(array, pltpu.HBM) for array in arrays]
    return call(prepare_kernel, shapes, scalars, arrays, (1 << 30, 3 << 20), spaces, scratch)


def operators_kernel(
    scalars, residual, near, far, maps_ref, adjusted, near_basis, far_basis, message, outer, extra, up_out
):
    columns = residual.shape[0]
    maps = maps_ref[...]
    first = scalars[0] == 0
    left = jnp.where(first, near[...], far[...])
    right = jnp.where(first, far[...], near[...])
    right = dot_t(right, placement(scalars[1])).astype(BF)
    near_basis[...] = jnp.where(first, left[columns:], right[columns:])
    far_basis[...] = jnp.where(first, right[columns:], left[columns:])
    adjusted[...] = residual[...]
    adjusted[:, :KMAX] = residual[:, :KMAX] - 0.5 * left[:columns].astype(F32)
    adjusted[:, M - KMAX :] = residual[:, M - KMAX :] - 0.5 * right[:columns].astype(F32)
    terms = dot_t(adjusted[...].astype(BF), maps)
    from_left = (0.5 * dot_t(left[columns:], maps[:, :KMAX])).astype(BF)
    from_right = (0.5 * dot_t(right[columns:], maps[:, M - KMAX :])).astype(BF)
    from_near = jnp.where(first, from_left, from_right)
    from_far = jnp.where(first, from_right, from_left)

    def stack(inputs, outputs, own):
        turned = (-own.astype(F32)).T.astype(BF)
        return jnp.concatenate([from_near[inputs, outputs], turned, from_far[inputs, outputs]], axis=0)

    down, up = slice(0, FACE), slice(FACE, 2 * FACE)
    down_down = stack(down, down, maps[:FACE, :FACE])
    down_up = stack(down, up, maps[FACE:, :FACE])
    up_up = stack(up, up, maps[FACE:, M - FACE :])
    down0 = terms[:, :FACE].astype(BF)
    message[:columns] = down0
    message[columns:] = jnp.where(first, down_down, up_up)
    outer[:columns] = down0
    outer[columns:] = jnp.where(first, up_up, down_down)
    extra[:columns] = terms[:, FACE:].astype(BF)
    extra[columns:] = down_up
    up_out[...] = terms[:, FACE:]


def local_operators(scalars, residual, near, far, maps):
    columns = residual.shape[0]
    pack, basis = ((columns + 3 * FACE, FACE), BF), ((2 * FACE, KMAX), BF)
    shapes = [((columns, M), F32), basis, basis, pack, pack, pack, ((columns, FACE), F32)]
    return call(operators_kernel, shapes, scalars, [residual, near, far, maps], (1 << 28, 3 << 20))


def block(array, at):
    return array[at * FACE : (at + 1) * FACE]


def turned(rows):
    return jnp.concatenate([block(rows, 2), block(rows, 1), block(rows, 0)], axis=0)


def compose(rows3, last, width):
    products = [dot(rows3[m], block(last, m)) for m in range(3)]
    return [sum(block(products[m], at - m) for m in range(3) if 0 <= at - m < width) for at in range(width + 2)]


def share_kernel(
    scalars, near, own, far, outer, outer_o, extra, extra_o, up0,
    forward, backward, reach, reach_start, even_rows, odd_rows, even_down, turn, even_start,
):
    columns = up0.shape[0]
    end = columns + 3 * FACE
    first = scalars[0] == 0

    def split(mine, other):
        a, b = mine[columns:], turned(other[columns:])
        return jnp.where(first, a, b), jnp.where(first, b, a)

    even3 = [near[columns:end], own[columns:end], turned(far[columns:end])]
    odd3 = [near[end:], own[end:], turned(far[end:])]
    even_up, odd_down = split(outer, outer_o)
    even_mixed, odd_mixed = split(extra, extra_o)
    down3 = jnp.concatenate([near[:columns], own[:columns], far[:columns]], axis=1)
    even_down[...] = down3
    for at in range(3):
        even_rows[at * 3 * FACE : (at + 1) * 3 * FACE] = even3[at]
        odd_rows[at * 3 * FACE : (at + 1) * 3 * FACE] = odd3[at]
    forward[...] = jnp.concatenate(compose(even3, odd_down, 3), axis=0).astype(BF)
    backward[...] = jnp.concatenate(compose(odd3, even_up, 3), axis=0).astype(BF)
    up_other = extra_o[:columns].astype(F32)
    odd_start = jnp.where(first, up_other, up0[...]) + dot(down3, odd_mixed)
    reach_start[...] = odd_start
    reach[:columns] = odd_start.astype(BF)
    reach[columns:] = jnp.concatenate(compose(even3, odd_mixed, 3), axis=0).astype(BF)
    turn[: 3 * FACE] = even_mixed
    turn[3 * FACE :] = even_up
    even_start[...] = jnp.where(first, up0[...], up_other)


def turn_kernel(scalars, near, own, far, turn, even_start, operator, start):
    columns = even_start.shape[0]
    last = turn[3 * FACE :]
    far_rows = jnp.concatenate([block(far[columns:], at) for at in range(4, -1, -1)], axis=0)
    wide = compose([near[columns:], own[columns:], far_rows], last, 5)
    mixed = [block(turn, at).astype(F32) for at in range(3)]
    wide = [wide[at] + mixed[at - 2] if 2 <= at < 5 else wide[at] for at in range(7)]
    operator[...] = jnp.concatenate(wide, axis=0).astype(BF)
    rows = jnp.concatenate([near[:columns], own[:columns], far[:columns]], axis=1)
    start[...] = jnp.where(scalars[0] == 0, even_start[...] + dot(rows, last), 0.0)


def five(mine, other):
    own = mine[:, 2 * FACE :] + other[:, 2 * FACE :]
    return jnp.concatenate([mine[:, : 2 * FACE], own, other[:, FACE : 2 * FACE], other[:, :FACE]], axis=1)


def between(base3, faces5, rows):
    found = []
    for m in range(3):
        part = slice(m * FACE, (m + 1) * FACE)
        reach = slice(m * FACE, (m + 3) * FACE)
        inside = rows[m * 3 * FACE : (m + 1) * 3 * FACE]
        found.append((base3[:, part].astype(F32) + dot(faces5[:, reach], inside)).astype(BF))
    return jnp.concatenate(found, axis=1)


def faces_kernel(scalars, mine, other, even_down, even_rows, down):
    faces = five(mine, other)
    inside = between(even_down[...], faces, even_rows[...])
    down[...] = jnp.where(scalars[0] == 0, faces[:, FACE : 4 * FACE], inside)


def settle_kernel(scalars, adjusted, near_basis, far_basis, down, near, own, far, odd_rows, factor_ref, out, operator):
    first = scalars[0] == 0
    factor = factor_ref[...]
    columns = out.shape[0]
    up3 = jnp.concatenate([near[...], own[...], far[...]], axis=1)
    up = jnp.where(first, up3, jnp.zeros_like(up3))

    def side(at, basis):
        part = slice(at * FACE, (at + 1) * FACE)
        return 0.5 * dot(jnp.concatenate([down[:, part], up[:, part]], axis=1), basis[...])

    middle = slice(FACE, 2 * FACE)
    near_side, far_side = side(0, near_basis), side(2, far_basis)
    low = adjusted[:, :KMAX] + jnp.where(first, near_side, far_side)
    high = adjusted[:, M - KMAX :] + jnp.where(first, far_side, near_side)
    rows = jnp.concatenate(
        [
            (low[:, :FACE] - down[:, middle].astype(F32)).astype(BF),
            low[:, FACE:].astype(BF),
            adjusted[:, KMAX : M - KMAX].astype(BF),
            high[:, : KMAX - FACE].astype(BF),
            (high[:, KMAX - FACE :] - up[:, middle].astype(F32)).astype(BF),
        ],
        axis=1,
    )

    zero = jnp.zeros((FACE, FACE), BF)
    one = jnp.where(
        lax.broadcasted_iota(jnp.int32, (FACE, FACE), 0) == lax.broadcasted_iota(jnp.int32, (FACE, FACE), 1), 1.0, 0.0
    ).astype(BF)
    ends = [[], [], []]
    for at in range(5):
        for m in range(3):
            inside = odd_rows[(m * 3 + at - m) * FACE : (m * 3 + at - m + 1) * FACE] if 0 <= at - m < 3 else zero
            ends[m].append(jnp.where(first, inside, one if at == m + 1 else zero))
    ends = [jnp.concatenate(blocks, axis=0) for blocks in ends]
    near_end = 0.5 * dot(ends[0], near_basis[FACE:])
    far_end = 0.5 * dot(ends[2], far_basis[FACE:])
    low = jnp.where(first, near_end, far_end)
    high = jnp.where(first, far_end, near_end)
    high = high - jnp.concatenate([jnp.zeros_like(ends[1]), ends[1]], axis=1).astype(F32)
    gap = jnp.zeros((5 * FACE, M - 2 * KMAX), BF)
    change = jnp.concatenate([low.astype(BF), gap, high.astype(BF)], axis=1)
    half = halves(jnp.concatenate([rows, change], axis=0), factor)
    for at in range(0, M, KMAX):
        block_out = dot(half[:, at:], factor[at:, at : at + KMAX])
        out[:, at : at + KMAX] = block_out[:columns]
        operator[:, at : at + KMAX] = block_out[columns:].astype(BF)


def on_device(right_side, inverse_factor, forward_trace, backward_trace, margin):
    slabs = lax.axis_size("slab")
    patches = lax.axis_size("patch")
    chips = slabs // 2

    def place(slab, patch):
        return slab * patches + patch % patches

    everywhere = [(slab, patch) for slab in range(slabs) for patch in range(patches)]

    def send(value, pairs):
        return lax.ppermute(value, AXES, pairs)

    def swap(value):
        return send(value, [(place(s, q), place(s ^ 1, q)) for s, q in everywhere])

    def from_near(value):
        return send(value, [(place(s, q), place(s, q + (-1) ** s)) for s, q in everywhere])

    def from_far(value):
        return send(value, [(place(s, q), place(s, q - (-1) ** s)) for s, q in everywhere])

    def hop(value, chip, step, width):
        shift = 2 * step
        arrived = []
        for by in range(width, -1, -1):
            pairs = []
            for slab in (2 * chip, 2 * chip + 1)[: 2 if by else 1]:
                pairs += [(place(slab, q), place(slab + shift, q + by * (-1) ** slab)) for q in range(patches)]
            arrived.append(send(value, pairs))
        return arrived

    core = lax.axis_index("slab") % 2
    first = core == 0
    def pick(on_first, on_second):
        return jnp.where(first, on_first, on_second)

    last_chip = lax.axis_index("slab") // 2 == chips - 1
    residual = right_side[0, 0]
    factor = inverse_factor[0, 0]
    columns = residual.shape[0]
    scalars = jnp.stack([core.astype(jnp.int32), margin[0, 0], last_chip.astype(jnp.int32)])
    face = (columns, FACE)
    three, five_, seven = 3 * FACE, 5 * FACE, 7 * FACE

    to_near, to_far, maps = prepare(scalars, residual, factor, forward_trace[0, 0], backward_trace[0, 0])
    near, far = from_near(to_near), from_far(to_far)
    adjusted, near_basis, far_basis, message, outer, extra, up0 = local_operators(
        scalars, residual, near, far, maps
    )

    message_other = swap(message)
    outer_other = swap(outer)
    mine, other = message[columns:], turned(message_other[columns:])
    pack = jnp.concatenate(
        [pick(message[:columns], message_other[:columns]), pick(mine, other), pick(other, mine)], axis=0
    )
    near = from_near(pack)

    def joined(part):
        return (part + swap(part)).astype(BF)

    nothing = jnp.zeros(face, F32)
    odd_down = pick(turned(outer_other[columns:]), outer[columns:])
    own_down = pick(pack[:columns], jnp.zeros(face, BF))
    base = dot(jnp.concatenate([near[:columns], own_down], axis=1), odd_down[: 2 * FACE])
    base = base + pick(outer_other[:columns].astype(F32), nothing)
    pieces = hop(joined(base), 0, 1, 2)

    far, extra_other = swap(near), swap(extra)
    rows = ((3 * three, FACE), BF)
    band = ((five_, FACE), BF)
    forward, backward, reach, reach_start, even_rows, odd_rows, even_down, turn, even_start = call(
        share_kernel,
        [band, band, ((columns + five_, FACE), BF), (face, F32), rows, rows, ((columns, three), BF),
         ((2 * three, FACE), BF), (face, F32)],
        scalars,
        [near, pack, far, outer, outer_other, extra, extra_other, up0],
        (1 << 10, 1 << 10),
    )

    def step(pieces, base, operator, *later, beside=()):
        pieces, base, operator, later, beside = barrier((pieces, base, operator, later, list(beside)))
        rows = jnp.concatenate([*pieces, *beside], axis=1)
        part = base + dot(rows, operator[: rows.shape[1]])
        part, pieces, beside = barrier((part, pieces, beside))
        return joined(part), jnp.concatenate(pieces[-3:], axis=1), *later, *beside

    def inward(seen):
        return dot(seen, reach[columns : columns + three])

    barrier = lax.optimization_barrier
    total, seen = step(pieces, base, forward)
    pieces = hop(total, 1, 1, 2)
    reach_near = from_near(reach)
    total, new, reach_near, seen = step(pieces, base, forward, reach_near, seen)
    pieces = hop(total, 2, 1, 3)
    seen = seen + new
    reached = inward(seen)

    operator, even_turn = call(
        turn_kernel,
        [((seven, FACE), BF), (face, F32)],
        scalars,
        [reach_near, reach, swap(reach_near), turn, even_start],
        (1 << 10, 1 << 10),
    )
    reached_other = swap(reached)
    total, new, reached_other, operator = step(pieces, even_turn, operator, reached_other, operator)
    pieces = hop(total, 3, -1, 2)

    seen_all = seen + new
    reached_last = inward(new)
    last_other = swap(reached_last)
    reached_other, last_other = barrier((reached_other, last_other))
    own = (reach_start + reached + reached_other).astype(BF)
    near = from_near(own)
    own_part = jnp.concatenate([seen[:, FACE:], pick(own, jnp.zeros(face, BF))], axis=1)
    own_turn = jnp.concatenate([turn[: 2 * FACE], turn[4 * FACE : 5 * FACE]], axis=0)
    near_turn = turn[3 * FACE : 4 * FACE]
    base = pick(even_start, nothing) + dot(own_part, own_turn)
    turned_back = jnp.concatenate([backward[:three], near_turn], axis=0)
    total, seen, last_other, near = step(pieces, base, turned_back, last_other, beside=[near])
    pieces = hop(total, 2, -1, 2)
    base = base + dot(near, near_turn)

    own_last = (reach_start + reached_last + last_other).astype(BF)
    near_last = from_near(own_last)
    seen_other = swap(seen_all)
    down = call(
        faces_kernel, [((columns, three), BF)], scalars, [seen_all, seen_other, even_down, even_rows], (1 << 10, 1 << 10)
    )[0]
    total, new, near_last, down = step(pieces, base, backward, near_last, down)
    pieces = hop(total, 1, -1, 2)
    seen = seen + new
    near, own = jnp.where(last_chip, near_last, near), jnp.where(last_chip, own_last, own)
    settled, operator = call(
        settle_kernel,
        [((columns, M), F32), ((five_, M), BF)],
        scalars,
        [adjusted, near_basis, far_basis, down, near, own, swap(near), odd_rows, factor],
        (1 << 10, 1 << 10),
    )
    pieces, seen, operator = barrier((pieces, seen, operator))
    seen = seen + jnp.concatenate(pieces, axis=1)
    out = settled + dot(barrier(five(seen, swap(seen))), operator)
    return out[None, None]


def solution(mesh):
    placed = (
        P("slab", "patch", None, None),
        P("slab", "patch", None, None),
        P("slab", "patch", None, None),
        P("slab", "patch", None, None),
        P("slab", "patch"),
    )
    return jax.shard_map(
        on_device,
        mesh=mesh,
        in_specs=placed,
        out_specs=P("slab", "patch", None, None),
        check_vma=False,
    )
```

```python
import jax
import jax.numpy as jnp
from jax import lax
from jax.experimental import pallas as pl
from jax.experimental.pallas import tpu as pltpu
from jax.sharding import PartitionSpec as P

M = 768
KMAX = 256
FACE = 128
BF = jnp.bfloat16
F32 = jnp.float32
AXES = ("slab", "patch")
VMEM = pl.BlockSpec(memory_space=pltpu.VMEM)
SMEM = pl.BlockSpec(memory_space=pltpu.SMEM)


def dot(a, b):
    return lax.dot_general(a, b, (((1,), (0,)), ((), ())), preferred_element_type=F32)


def dot_t(a, b):
    return lax.dot_general(a, b, (((1,), (1,)), ((), ())), preferred_element_type=F32)


def placement(limit):
    source = lax.broadcasted_iota(jnp.int32, (KMAX, KMAX), 0)
    target = lax.broadcasted_iota(jnp.int32, (KMAX, KMAX), 1)
    hit = (source == KMAX - limit + target) & (target < limit)
    return jnp.where(hit, 1.0, 0.0).astype(BF)


def halves(rows, factor):
    found = []
    for at in range(0, M, KMAX):
        end = at + KMAX
        found.append(dot_t(rows[:, :end], factor[at:end, :end]).astype(BF))
    return jnp.concatenate(found, axis=1)


def call(kernel, shapes, scalars, arrays, cost, spaces=None, scratch=()):
    return pl.pallas_call(
        kernel,
        out_shape=[jax.ShapeDtypeStruct(shape, kind) for shape, kind in shapes],
        in_specs=[SMEM] + (spaces or [VMEM] * len(arrays)),
        out_specs=[VMEM] * len(shapes),
        scratch_shapes=list(scratch),
        cost_estimate=pl.CostEstimate(flops=cost[0], bytes_accessed=cost[1], transcendentals=0),
        compiler_params=pltpu.CompilerParams(vmem_limit_bytes=40 << 20),
    )(scalars, *arrays)


def prepare_kernel(
    scalars, residual_in, factor_in, down_in, up_in, near, far, maps, residual, factor, down_map, up_map, sems
):
    last = M - KMAX
    parts = [
        (factor_in.at[:KMAX, :KMAX], factor.at[:KMAX, :KMAX]),
        (factor_in.at[KMAX:last, :last], factor.at[KMAX:last, :last]),
        (factor_in.at[last:], factor.at[last:]),
        (down_in, down_map),
        (up_in, up_map),
    ]
    for at in range(0, M, KMAX):
        parts.append((residual_in.at[:, at : at + KMAX], residual.at[:, at : at + KMAX]))
    copies = [pltpu.make_async_copy(source, target, sems.at[at]) for at, (source, target) in enumerate(parts)]
    for copy in copies:
        copy.start()
    columns = residual.shape[0]
    first = scalars[0] == 0
    for copy in copies[:3]:
        copy.wait()
    low = factor[:, :FACE].T
    high = factor[M - FACE :, M - FACE :].T
    low_head = dot(low, factor[:, :KMAX]).astype(BF)
    high_head = dot(high, factor[M - FACE :, :KMAX]).astype(BF)
    low_tail = dot(low[:, last:], factor[last:, last:]).astype(BF)
    high_tail = dot(high, factor[M - FACE :, last:]).astype(BF)
    copies[3].wait()
    copies[4].wait()
    rows, half = [], []
    for at in range(3):
        copies[5 + at].wait()
        where = slice(at * KMAX, (at + 1) * KMAX)
        rows.append(jnp.concatenate([residual[:, where].astype(BF), down_map[:, where], up_map[:, where]], axis=0))
        known = jnp.concatenate(rows, axis=1)
        half.append(dot_t(known, factor[where, : known.shape[1]]).astype(BF))
    half2 = half[2]
    half = jnp.concatenate(half, axis=1)
    first_block = dot(half, factor[:, :KMAX]).astype(BF)
    last_block = dot(half2, factor[last:, last:]).astype(BF)
    middle_block = dot(half[columns:, KMAX:], factor[KMAX:, KMAX:last]).astype(BF)
    head = jnp.concatenate([first_block[:columns], low_head, high_head], axis=0)
    ends = jnp.concatenate([last_block[:columns], low_tail, high_tail], axis=0)
    tail = dot(ends, placement(scalars[1])).astype(BF)
    near[...] = jnp.where(first, tail, head)
    far[...] = jnp.where(first, head, tail)
    maps[:, :KMAX] = first_block[columns:]
    maps[:, KMAX:last] = middle_block
    maps[:, last:] = last_block[columns:]


def prepare(scalars, residual, factor, down_map, up_map):
    columns = residual.shape[0]
    reach = columns + 2 * FACE
    shapes = [((reach, KMAX), BF), ((reach, KMAX), BF), ((2 * FACE, M), BF)]
    arrays = [residual, factor, down_map, up_map]
    scratch = [pltpu.VMEM(array.shape, array.dtype) for array in arrays] + [pltpu.SemaphoreType.DMA((8,))]
    spaces = [pl.BlockSpec(memory_space=pltpu.HBM)] * 4
    arrays = [pltpu.with_memory_space_constraint(array, pltpu.HBM) for array in arrays]
    return call(prepare_kernel, shapes, scalars, arrays, (1 << 30, 3 << 20), spaces, scratch)


def operators_kernel(
    scalars, residual, near, far, maps_ref, adjusted, near_basis, far_basis, message, outer, extra, up_out
):
    columns = residual.shape[0]
    maps = maps_ref[...]
    first = scalars[0] == 0
    left = jnp.where(first, near[...], far[...])
    right = jnp.where(first, far[...], near[...])
    right = dot_t(right, placement(scalars[1])).astype(BF)
    near_basis[...] = jnp.where(first, left[columns:], right[columns:])
    far_basis[...] = jnp.where(first, right[columns:], left[columns:])
    adjusted[...] = residual[...]
    adjusted[:, :KMAX] = residual[:, :KMAX] - 0.5 * left[:columns].astype(F32)
    adjusted[:, M - KMAX :] = residual[:, M - KMAX :] - 0.5 * right[:columns].astype(F32)
    terms = dot_t(adjusted[...].astype(BF), maps)
    from_left = (0.5 * dot_t(left[columns:], maps[:, :KMAX])).astype(BF)
    from_right = (0.5 * dot_t(right[columns:], maps[:, M - KMAX :])).astype(BF)
    from_near = jnp.where(first, from_left, from_right)
    from_far = jnp.where(first, from_right, from_left)

    def stack(inputs, outputs, own):
        turned = (-own.astype(F32)).T.astype(BF)
        return jnp.concatenate([from_near[inputs, outputs], turned, from_far[inputs, outputs]], axis=0)

    down, up = slice(0, FACE), slice(FACE, 2 * FACE)
    down_down = stack(down, down, maps[:FACE, :FACE])
    down_up = stack(down, up, maps[FACE:, :FACE])
    up_up = stack(up, up, maps[FACE:, M - FACE :])
    down0 = terms[:, :FACE].astype(BF)
    message[:columns] = down0
    message[columns:] = jnp.where(first, down_down, up_up)
    outer[:columns] = down0
    outer[columns:] = jnp.where(first, up_up, down_down)
    extra[:columns] = terms[:, FACE:].astype(BF)
    extra[columns:] = down_up
    up_out[...] = terms[:, FACE:]


def local_operators(scalars, residual, near, far, maps):
    columns = residual.shape[0]
    pack, basis = ((columns + 3 * FACE, FACE), BF), ((2 * FACE, KMAX), BF)
    shapes = [((columns, M), F32), basis, basis, pack, pack, pack, ((columns, FACE), F32)]
    return call(operators_kernel, shapes, scalars, [residual, near, far, maps], (1 << 28, 3 << 20))


def block(array, at):
    return array[at * FACE : (at + 1) * FACE]


def turned(rows):
    return jnp.concatenate([block(rows, 2), block(rows, 1), block(rows, 0)], axis=0)


def compose(rows3, last, width):
    products = [dot(rows3[m], block(last, m)) for m in range(3)]
    return [sum(block(products[m], at - m) for m in range(3) if 0 <= at - m < width) for at in range(width + 2)]


def share_kernel(
    scalars, near, own, far, outer, outer_o, extra, extra_o, up0,
    forward, backward, reach, reach_start, even_rows, odd_rows, even_down, turn, even_start,
):
    columns = up0.shape[0]
    end = columns + 3 * FACE
    first = scalars[0] == 0

    def split(mine, other):
        a, b = mine[columns:], turned(other[columns:])
        return jnp.where(first, a, b), jnp.where(first, b, a)

    even3 = [near[columns:end], own[columns:end], turned(far[columns:end])]
    odd3 = [near[end:], own[end:], turned(far[end:])]
    even_up, odd_down = split(outer, outer_o)
    even_mixed, odd_mixed = split(extra, extra_o)
    down3 = jnp.concatenate([near[:columns], own[:columns], far[:columns]], axis=1)
    even_down[...] = down3
    for at in range(3):
        even_rows[at * 3 * FACE : (at + 1) * 3 * FACE] = even3[at]
        odd_rows[at * 3 * FACE : (at + 1) * 3 * FACE] = odd3[at]
    forward[...] = jnp.concatenate(compose(even3, odd_down, 3), axis=0).astype(BF)
    backward[...] = jnp.concatenate(compose(odd3, even_up, 3), axis=0).astype(BF)
    up_other = extra_o[:columns].astype(F32)
    odd_start = jnp.where(first, up_other, up0[...]) + dot(down3, odd_mixed)
    reach_start[...] = odd_start
    reach[:columns] = odd_start.astype(BF)
    reach[columns:] = jnp.concatenate(compose(even3, odd_mixed, 3), axis=0).astype(BF)
    turn[: 3 * FACE] = even_mixed
    turn[3 * FACE :] = even_up
    even_start[...] = jnp.where(first, up0[...], up_other)


def turn_kernel(scalars, near, own, far, turn, even_start, operator, start):
    columns = even_start.shape[0]
    last = turn[3 * FACE :]
    far_rows = jnp.concatenate([block(far[columns:], at) for at in range(4, -1, -1)], axis=0)
    wide = compose([near[columns:], own[columns:], far_rows], last, 5)
    mixed = [block(turn, at).astype(F32) for at in range(3)]
    wide = [wide[at] + mixed[at - 2] if 2 <= at < 5 else wide[at] for at in range(7)]
    operator[...] = jnp.concatenate(wide, axis=0).astype(BF)
    rows = jnp.concatenate([near[:columns], own[:columns], far[:columns]], axis=1)
    start[...] = jnp.where(scalars[0] == 0, even_start[...] + dot(rows, last), 0.0)


def five(mine, other):
    own = mine[:, 2 * FACE :] + other[:, 2 * FACE :]
    return jnp.concatenate([mine[:, : 2 * FACE], own, other[:, FACE : 2 * FACE], other[:, :FACE]], axis=1)


def between(base3, faces5, rows):
    found = []
    for m in range(3):
        part = slice(m * FACE, (m + 1) * FACE)
        reach = slice(m * FACE, (m + 3) * FACE)
        inside = rows[m * 3 * FACE : (m + 1) * 3 * FACE]
        found.append((base3[:, part].astype(F32) + dot(faces5[:, reach], inside)).astype(BF))
    return jnp.concatenate(found, axis=1)


def faces_kernel(scalars, mine, other, even_down, even_rows, down):
    faces = five(mine, other)
    inside = between(even_down[...], faces, even_rows[...])
    down[...] = jnp.where(scalars[0] == 0, faces[:, FACE : 4 * FACE], inside)


def settle_kernel(scalars, adjusted, near_basis, far_basis, down, near, own, far, odd_rows, factor_ref, out, operator):
    first = scalars[0] == 0
    factor = factor_ref[...]
    columns = out.shape[0]
    up3 = jnp.concatenate([near[...], own[...], far[...]], axis=1)
    up = jnp.where(first, up3, jnp.zeros_like(up3))

    def side(at, basis):
        part = slice(at * FACE, (at + 1) * FACE)
        return 0.5 * dot(jnp.concatenate([down[:, part], up[:, part]], axis=1), basis[...])

    middle = slice(FACE, 2 * FACE)
    near_side, far_side = side(0, near_basis), side(2, far_basis)
    low = adjusted[:, :KMAX] + jnp.where(first, near_side, far_side)
    high = adjusted[:, M - KMAX :] + jnp.where(first, far_side, near_side)
    rows = jnp.concatenate(
        [
            (low[:, :FACE] - down[:, middle].astype(F32)).astype(BF),
            low[:, FACE:].astype(BF),
            adjusted[:, KMAX : M - KMAX].astype(BF),
            high[:, : KMAX - FACE].astype(BF),
            (high[:, KMAX - FACE :] - up[:, middle].astype(F32)).astype(BF),
        ],
        axis=1,
    )

    zero = jnp.zeros((FACE, FACE), BF)
    one = jnp.where(
        lax.broadcasted_iota(jnp.int32, (FACE, FACE), 0) == lax.broadcasted_iota(jnp.int32, (FACE, FACE), 1), 1.0, 0.0
    ).astype(BF)
    ends = [[], [], []]
    for at in range(5):
        for m in range(3):
            inside = odd_rows[(m * 3 + at - m) * FACE : (m * 3 + at - m + 1) * FACE] if 0 <= at - m < 3 else zero
            ends[m].append(jnp.where(first, inside, one if at == m + 1 else zero))
    ends = [jnp.concatenate(blocks, axis=0) for blocks in ends]
    near_end = 0.5 * dot(ends[0], near_basis[FACE:])
    far_end = 0.5 * dot(ends[2], far_basis[FACE:])
    low = jnp.where(first, near_end, far_end)
    high = jnp.where(first, far_end, near_end)
    high = high - jnp.concatenate([jnp.zeros_like(ends[1]), ends[1]], axis=1).astype(F32)
    gap = jnp.zeros((5 * FACE, M - 2 * KMAX), BF)
    change = jnp.concatenate([low.astype(BF), gap, high.astype(BF)], axis=1)
    half = halves(jnp.concatenate([rows, change], axis=0), factor)
    for at in range(0, M, KMAX):
        block_out = dot(half[:, at:], factor[at:, at : at + KMAX])
        out[:, at : at + KMAX] = block_out[:columns]
        operator[:, at : at + KMAX] = block_out[columns:].astype(BF)


def on_device(right_side, inverse_factor, forward_trace, backward_trace, margin):
    slabs = lax.axis_size("slab")
    patches = lax.axis_size("patch")
    chips = slabs // 2

    def place(slab, patch):
        return slab * patches + patch % patches

    everywhere = [(slab, patch) for slab in range(slabs) for patch in range(patches)]

    def send(value, pairs):
        return lax.ppermute(value, AXES, pairs)

    def swap(value):
        return send(value, [(place(s, q), place(s ^ 1, q)) for s, q in everywhere])

    def from_near(value):
        return send(value, [(place(s, q), place(s, q + (-1) ** s)) for s, q in everywhere])

    def from_far(value):
        return send(value, [(place(s, q), place(s, q - (-1) ** s)) for s, q in everywhere])

    def hop(value, chip, step, width):
        shift = 2 * step
        arrived = []
        for by in range(width, -1, -1):
            pairs = []
            for slab in (2 * chip, 2 * chip + 1)[: 2 if by else 1]:
                pairs += [(place(slab, q), place(slab + shift, q + by * (-1) ** slab)) for q in range(patches)]
            arrived.append(send(value, pairs))
        return arrived

    core = lax.axis_index("slab") % 2
    first = core == 0
    def pick(on_first, on_second):
        return jnp.where(first, on_first, on_second)

    last_chip = lax.axis_index("slab") // 2 == chips - 1
    residual = right_side[0, 0]
    factor = inverse_factor[0, 0]
    columns = residual.shape[0]
    scalars = jnp.stack([core.astype(jnp.int32), margin[0, 0], last_chip.astype(jnp.int32)])
    face = (columns, FACE)
    three, five_, seven = 3 * FACE, 5 * FACE, 7 * FACE

    to_near, to_far, maps = prepare(scalars, residual, factor, forward_trace[0, 0], backward_trace[0, 0])
    near, far = from_near(to_near), from_far(to_far)
    adjusted, near_basis, far_basis, message, outer, extra, up0 = local_operators(
        scalars, residual, near, far, maps
    )

    message_other = swap(message)
    outer_other = swap(outer)
    mine, other = message[columns:], turned(message_other[columns:])
    pack = jnp.concatenate(
        [pick(message[:columns], message_other[:columns]), pick(mine, other), pick(other, mine)], axis=0
    )
    near = from_near(pack)

    def joined(part):
        return (part + swap(part)).astype(BF)

    nothing = jnp.zeros(face, F32)
    odd_down = pick(turned(outer_other[columns:]), outer[columns:])
    own_down = pick(pack[:columns], jnp.zeros(face, BF))
    base = dot(jnp.concatenate([near[:columns], own_down], axis=1), odd_down[: 2 * FACE])
    base = base + pick(outer_other[:columns].astype(F32), nothing)
    pieces = hop(joined(base), 0, 1, 2)

    far, extra_other = swap(near), swap(extra)
    rows = ((3 * three, FACE), BF)
    band = ((five_, FACE), BF)
    forward, backward, reach, reach_start, even_rows, odd_rows, even_down, turn, even_start = call(
        share_kernel,
        [band, band, ((columns + five_, FACE), BF), (face, F32), rows, rows, ((columns, three), BF),
         ((2 * three, FACE), BF), (face, F32)],
        scalars,
        [near, pack, far, outer, outer_other, extra, extra_other, up0],
        (1 << 10, 1 << 10),
    )

    def step(pieces, base, operator, *later, beside=()):
        pieces, base, operator, later, beside = barrier((pieces, base, operator, later, list(beside)))
        rows = jnp.concatenate([*pieces, *beside], axis=1)
        part = base + dot(rows, operator[: rows.shape[1]])
        part, pieces, beside = barrier((part, pieces, beside))
        return joined(part), jnp.concatenate(pieces[-3:], axis=1), *later, *beside

    def inward(seen):
        return dot(seen, reach[columns : columns + three])

    barrier = lax.optimization_barrier
    total, seen = step(pieces, base, forward)
    pieces = hop(total, 1, 1, 2)
    reach_near = from_near(reach)
    total, new, reach_near, seen = step(pieces, base, forward, reach_near, seen)
    pieces = hop(total, 2, 1, 3)
    seen = seen + new
    reached = inward(seen)

    operator, even_turn = call(
        turn_kernel,
        [((seven, FACE), BF), (face, F32)],
        scalars,
        [reach_near, reach, swap(reach_near), turn, even_start],
        (1 << 10, 1 << 10),
    )
    reached_other = swap(reached)
    total, new, reached_other, operator = step(pieces, even_turn, operator, reached_other, operator)
    pieces = hop(total, 3, -1, 2)

    seen_all = seen + new
    reached_last = inward(new)
    last_other = swap(reached_last)
    reached_other, last_other = barrier((reached_other, last_other))
    own = (reach_start + reached + reached_other).astype(BF)
    near = from_near(own)
    own_part = jnp.concatenate([seen[:, FACE:], pick(own, jnp.zeros(face, BF))], axis=1)
    own_turn = jnp.concatenate([turn[: 2 * FACE], turn[4 * FACE : 5 * FACE]], axis=0)
    near_turn = turn[3 * FACE : 4 * FACE]
    base = pick(even_start, nothing) + dot(own_part, own_turn)
    turned_back = jnp.concatenate([backward[:three], near_turn], axis=0)
    total, seen, last_other, near = step(pieces, base, turned_back, last_other, beside=[near])
    pieces = hop(total, 2, -1, 2)
    base = base + dot(near, near_turn)

    own_last = (reach_start + reached_last + last_other).astype(BF)
    near_last = from_near(own_last)
    seen_other = swap(seen_all)
    down = call(
        faces_kernel, [((columns, three), BF)], scalars, [seen_all, seen_other, even_down, even_rows], (1 << 10, 1 << 10)
    )[0]
    total, new, near_last, down = step(pieces, base, backward, near_last, down)
    pieces = hop(total, 1, -1, 2)
    seen = seen + new
    near, own = jnp.where(last_chip, near_last, near), jnp.where(last_chip, own_last, own)
    settled, operator = call(
        settle_kernel,
        [((columns, M), F32), ((five_, M), BF)],
        scalars,
        [adjusted, near_basis, far_basis, down, near, own, swap(near), odd_rows, factor],
        (1 << 10, 1 << 10),
    )
    pieces, seen, operator = barrier((pieces, seen, operator))
    seen = seen + jnp.concatenate(pieces, axis=1)
    out = settled + dot(barrier(five(seen, swap(seen))), operator)
    return out[None, None]


def solution(mesh):
    placed = (
        P("slab", "patch", None, None),
        P("slab", "patch", None, None),
        P("slab", "patch", None, None),
        P("slab", "patch", None, None),
        P("slab", "patch"),
    )
    return jax.shard_map(
        on_device,
        mesh=mesh,
        in_specs=placed,
        out_specs=P("slab", "patch", None, None),
        check_vma=False,
    )
```

```python
import jax
import jax.numpy as jnp
from jax import lax
from jax.experimental import pallas as pl
from jax.experimental.pallas import tpu as pltpu
from jax.sharding import PartitionSpec as P

M = 768
KMAX = 256
FACE = 128
BF = jnp.bfloat16
F32 = jnp.float32
AXES = ("slab", "patch")
VMEM = pl.BlockSpec(memory_space=pltpu.VMEM)
SMEM = pl.BlockSpec(memory_space=pltpu.SMEM)


def dot(a, b):
    return lax.dot_general(a, b, (((1,), (0,)), ((), ())), preferred_element_type=F32)


def dot_t(a, b):
    return lax.dot_general(a, b, (((1,), (1,)), ((), ())), preferred_element_type=F32)


def placement(limit):
    source = lax.broadcasted_iota(jnp.int32, (KMAX, KMAX), 0)
    target = lax.broadcasted_iota(jnp.int32, (KMAX, KMAX), 1)
    hit = (source == KMAX - limit + target) & (target < limit)
    return jnp.where(hit, 1.0, 0.0).astype(BF)


def halves(rows, factor):
    found = []
    for at in range(0, M, KMAX):
        end = at + KMAX
        found.append(dot_t(rows[:, :end], factor[at:end, :end]).astype(BF))
    return jnp.concatenate(found, axis=1)


def call(kernel, shapes, scalars, arrays, cost, spaces=None, scratch=()):
    return pl.pallas_call(
        kernel,
        out_shape=[jax.ShapeDtypeStruct(shape, kind) for shape, kind in shapes],
        in_specs=[SMEM] + (spaces or [VMEM] * len(arrays)),
        out_specs=[VMEM] * len(shapes),
        scratch_shapes=list(scratch),
        cost_estimate=pl.CostEstimate(flops=cost[0], bytes_accessed=cost[1], transcendentals=0),
        compiler_params=pltpu.CompilerParams(vmem_limit_bytes=40 << 20),
    )(scalars, *arrays)


def prepare_kernel(
    scalars, residual_in, factor_in, down_in, up_in, near, far, maps, residual, factor, down_map, up_map, sems
):
    last = M - KMAX
    copies = [
        pltpu.make_async_copy(source, target, sems.at[at])
        for at, (source, target) in enumerate(
            [
                (residual_in, residual),
                (down_in, down_map),
                (up_in, up_map),
                (factor_in.at[:KMAX, :KMAX], factor.at[:KMAX, :KMAX]),
                (factor_in.at[KMAX:last, :last], factor.at[KMAX:last, :last]),
                (factor_in.at[last:], factor.at[last:]),
            ]
        )
    ]
    for copy in copies:
        copy.start()
    columns = residual.shape[0]
    first = scalars[0] == 0
    for copy in copies[:4]:
        copy.wait()
    rows = jnp.concatenate([residual[...].astype(BF), down_map[...], up_map[...]], axis=0)
    half0 = dot_t(rows[:, :KMAX], factor[:KMAX, :KMAX]).astype(BF)
    copies[4].wait()
    half1 = dot_t(rows[:, :last], factor[KMAX:last, :last]).astype(BF)
    copies[5].wait()
    half2 = dot_t(rows, factor[last:, :]).astype(BF)
    half = jnp.concatenate([half0, half1, half2], axis=1)
    first_block = dot(half, factor[:, :KMAX]).astype(BF)
    last_block = dot(half2, factor[last:, last:]).astype(BF)
    middle_block = dot(half[columns:, KMAX:], factor[KMAX:, KMAX:last]).astype(BF)
    low = factor[:, :FACE].T
    high = factor[M - FACE :, M - FACE :].T
    head = jnp.concatenate(
        [
            first_block[:columns],
            dot(low, factor[:, :KMAX]).astype(BF),
            dot(high, factor[M - FACE :, :KMAX]).astype(BF),
        ],
        axis=0,
    )
    ends = jnp.concatenate(
        [
            last_block[:columns],
            dot(low[:, last:], factor[last:, last:]).astype(BF),
            dot(high, factor[M - FACE :, last:]).astype(BF),
        ],
        axis=0,
    )
    tail = dot(ends, placement(scalars[1])).astype(BF)
    near[...] = jnp.where(first, tail, head)
    far[...] = jnp.where(first, head, tail)
    maps[:, :KMAX] = first_block[columns:]
    maps[:, KMAX:last] = middle_block
    maps[:, last:] = last_block[columns:]


def prepare(scalars, residual, factor, down_map, up_map):
    columns = residual.shape[0]
    reach = columns + 2 * FACE
    shapes = [((reach, KMAX), BF), ((reach, KMAX), BF), ((2 * FACE, M), BF)]
    arrays = [residual, factor, down_map, up_map]
    scratch = [pltpu.VMEM(array.shape, array.dtype) for array in arrays] + [pltpu.SemaphoreType.DMA((6,))]
    spaces = [pl.BlockSpec(memory_space=pltpu.HBM)] * 4
    arrays = [pltpu.with_memory_space_constraint(array, pltpu.HBM) for array in arrays]
    return call(prepare_kernel, shapes, scalars, arrays, (1 << 30, 3 << 20), spaces, scratch)


def operators_kernel(
    scalars, residual, near, far, maps_ref, adjusted, near_basis, far_basis, message, outer, extra, up_out
):
    columns = residual.shape[0]
    maps = maps_ref[...]
    first = scalars[0] == 0
    left = jnp.where(first, near[...], far[...])
    right = jnp.where(first, far[...], near[...])
    right = dot_t(right, placement(scalars[1])).astype(BF)
    near_basis[...] = jnp.where(first, left[columns:], right[columns:])
    far_basis[...] = jnp.where(first, right[columns:], left[columns:])
    adjusted[...] = residual[...]
    adjusted[:, :KMAX] = residual[:, :KMAX] - 0.5 * left[:columns].astype(F32)
    adjusted[:, M - KMAX :] = residual[:, M - KMAX :] - 0.5 * right[:columns].astype(F32)
    terms = dot_t(adjusted[...].astype(BF), maps)
    from_left = (0.5 * dot_t(left[columns:], maps[:, :KMAX])).astype(BF)
    from_right = (0.5 * dot_t(right[columns:], maps[:, M - KMAX :])).astype(BF)
    from_near = jnp.where(first, from_left, from_right)
    from_far = jnp.where(first, from_right, from_left)

    def stack(inputs, outputs, own):
        turned = (-own.astype(F32)).T.astype(BF)
        return jnp.concatenate([from_near[inputs, outputs], turned, from_far[inputs, outputs]], axis=0)

    down, up = slice(0, FACE), slice(FACE, 2 * FACE)
    down_down = stack(down, down, maps[:FACE, :FACE])
    down_up = stack(down, up, maps[FACE:, :FACE])
    up_up = stack(up, up, maps[FACE:, M - FACE :])
    down0 = terms[:, :FACE].astype(BF)
    message[:columns] = down0
    message[columns:] = jnp.where(first, down_down, up_up)
    outer[:columns] = down0
    outer[columns:] = jnp.where(first, up_up, down_down)
    extra[:columns] = terms[:, FACE:].astype(BF)
    extra[columns:] = down_up
    up_out[...] = terms[:, FACE:]


def local_operators(scalars, residual, near, far, maps):
    columns = residual.shape[0]
    pack, basis = ((columns + 3 * FACE, FACE), BF), ((2 * FACE, KMAX), BF)
    shapes = [((columns, M), F32), basis, basis, pack, pack, pack, ((columns, FACE), F32)]
    return call(operators_kernel, shapes, scalars, [residual, near, far, maps], (1 << 28, 3 << 20))


def block(array, at):
    return array[at * FACE : (at + 1) * FACE]


def turned(rows):
    return jnp.concatenate([block(rows, 2), block(rows, 1), block(rows, 0)], axis=0)


def compose(rows3, last, width):
    products = [dot(rows3[m], block(last, m)) for m in range(3)]
    return [sum(block(products[m], at - m) for m in range(3) if 0 <= at - m < width) for at in range(width + 2)]


def share_kernel(
    scalars, near, own, far, outer, outer_o, extra, extra_o, up0,
    forward, backward, reach, reach_start, even_rows, odd_rows, even_down, turn, even_start,
):
    columns = up0.shape[0]
    end = columns + 3 * FACE
    first = scalars[0] == 0

    def split(mine, other):
        a, b = mine[columns:], turned(other[columns:])
        return jnp.where(first, a, b), jnp.where(first, b, a)

    even3 = [near[columns:end], own[columns:end], turned(far[columns:end])]
    odd3 = [near[end:], own[end:], turned(far[end:])]
    even_up, odd_down = split(outer, outer_o)
    even_mixed, odd_mixed = split(extra, extra_o)
    down3 = jnp.concatenate([near[:columns], own[:columns], far[:columns]], axis=1)
    even_down[...] = down3
    for at in range(3):
        even_rows[at * 3 * FACE : (at + 1) * 3 * FACE] = even3[at]
        odd_rows[at * 3 * FACE : (at + 1) * 3 * FACE] = odd3[at]
    forward[...] = jnp.concatenate(compose(even3, odd_down, 3), axis=0).astype(BF)
    backward[...] = jnp.concatenate(compose(odd3, even_up, 3), axis=0).astype(BF)
    up_other = extra_o[:columns].astype(F32)
    odd_start = jnp.where(first, up_other, up0[...]) + dot(down3, odd_mixed)
    reach_start[...] = odd_start
    reach[:columns] = odd_start.astype(BF)
    reach[columns:] = jnp.concatenate(compose(even3, odd_mixed, 3), axis=0).astype(BF)
    turn[: 3 * FACE] = even_mixed
    turn[3 * FACE :] = even_up
    even_start[...] = jnp.where(first, up0[...], up_other)


def turn_kernel(scalars, near, own, far, turn, even_start, operator, start):
    columns = even_start.shape[0]
    last = turn[3 * FACE :]
    far_rows = jnp.concatenate([block(far[columns:], at) for at in range(4, -1, -1)], axis=0)
    wide = compose([near[columns:], own[columns:], far_rows], last, 5)
    mixed = [block(turn, at).astype(F32) for at in range(3)]
    wide = [wide[at] + mixed[at - 2] if 2 <= at < 5 else wide[at] for at in range(7)]
    operator[...] = jnp.concatenate(wide, axis=0).astype(BF)
    rows = jnp.concatenate([near[:columns], own[:columns], far[:columns]], axis=1)
    start[...] = jnp.where(scalars[0] == 0, even_start[...] + dot(rows, last), 0.0)


def five(mine, other):
    own = mine[:, 2 * FACE :] + other[:, 2 * FACE :]
    return jnp.concatenate([mine[:, : 2 * FACE], own, other[:, FACE : 2 * FACE], other[:, :FACE]], axis=1)


def between(base3, faces5, rows):
    found = []
    for m in range(3):
        part = slice(m * FACE, (m + 1) * FACE)
        reach = slice(m * FACE, (m + 3) * FACE)
        inside = rows[m * 3 * FACE : (m + 1) * 3 * FACE]
        found.append((base3[:, part].astype(F32) + dot(faces5[:, reach], inside)).astype(BF))
    return jnp.concatenate(found, axis=1)


def faces_kernel(scalars, mine, other, even_down, even_rows, down):
    faces = five(mine, other)
    inside = between(even_down[...], faces, even_rows[...])
    down[...] = jnp.where(scalars[0] == 0, faces[:, FACE : 4 * FACE], inside)


def settle_kernel(scalars, adjusted, near_basis, far_basis, down, near, own, far, odd_rows, factor_ref, out, operator):
    first = scalars[0] == 0
    factor = factor_ref[...]
    columns = out.shape[0]
    up3 = jnp.concatenate([near[...], own[...], far[...]], axis=1)
    up = jnp.where(first, up3, jnp.zeros_like(up3))

    def side(at, basis):
        part = slice(at * FACE, (at + 1) * FACE)
        return 0.5 * dot(jnp.concatenate([down[:, part], up[:, part]], axis=1), basis[...])

    middle = slice(FACE, 2 * FACE)
    near_side, far_side = side(0, near_basis), side(2, far_basis)
    low = adjusted[:, :KMAX] + jnp.where(first, near_side, far_side)
    high = adjusted[:, M - KMAX :] + jnp.where(first, far_side, near_side)
    rows = jnp.concatenate(
        [
            (low[:, :FACE] - down[:, middle].astype(F32)).astype(BF),
            low[:, FACE:].astype(BF),
            adjusted[:, KMAX : M - KMAX].astype(BF),
            high[:, : KMAX - FACE].astype(BF),
            (high[:, KMAX - FACE :] - up[:, middle].astype(F32)).astype(BF),
        ],
        axis=1,
    )

    zero = jnp.zeros((FACE, FACE), BF)
    one = jnp.where(
        lax.broadcasted_iota(jnp.int32, (FACE, FACE), 0) == lax.broadcasted_iota(jnp.int32, (FACE, FACE), 1), 1.0, 0.0
    ).astype(BF)
    ends = [[], [], []]
    for at in range(5):
        for m in range(3):
            inside = odd_rows[(m * 3 + at - m) * FACE : (m * 3 + at - m + 1) * FACE] if 0 <= at - m < 3 else zero
            ends[m].append(jnp.where(first, inside, one if at == m + 1 else zero))
    ends = [jnp.concatenate(blocks, axis=0) for blocks in ends]
    near_end = 0.5 * dot(ends[0], near_basis[FACE:])
    far_end = 0.5 * dot(ends[2], far_basis[FACE:])
    low = jnp.where(first, near_end, far_end)
    high = jnp.where(first, far_end, near_end)
    high = high - jnp.concatenate([jnp.zeros_like(ends[1]), ends[1]], axis=1).astype(F32)
    gap = jnp.zeros((5 * FACE, M - 2 * KMAX), BF)
    change = jnp.concatenate([low.astype(BF), gap, high.astype(BF)], axis=1)
    half = halves(jnp.concatenate([rows, change], axis=0), factor)
    for at in range(0, M, KMAX):
        block_out = dot(half[:, at:], factor[at:, at : at + KMAX])
        out[:, at : at + KMAX] = block_out[:columns]
        operator[:, at : at + KMAX] = block_out[columns:].astype(BF)


def on_device(right_side, inverse_factor, forward_trace, backward_trace, margin):
    slabs = lax.axis_size("slab")
    patches = lax.axis_size("patch")
    chips = slabs // 2

    def place(slab, patch):
        return slab * patches + patch % patches

    everywhere = [(slab, patch) for slab in range(slabs) for patch in range(patches)]

    def send(value, pairs):
        return lax.ppermute(value, AXES, pairs)

    def swap(value):
        return send(value, [(place(s, q), place(s ^ 1, q)) for s, q in everywhere])

    def from_near(value):
        return send(value, [(place(s, q), place(s, q + (-1) ** s)) for s, q in everywhere])

    def from_far(value):
        return send(value, [(place(s, q), place(s, q - (-1) ** s)) for s, q in everywhere])

    def hop(value, chip, step, width):
        shift = 2 * step
        arrived = []
        for by in range(width, -1, -1):
            pairs = []
            for slab in (2 * chip, 2 * chip + 1)[: 2 if by else 1]:
                pairs += [(place(slab, q), place(slab + shift, q + by * (-1) ** slab)) for q in range(patches)]
            arrived.append(send(value, pairs))
        return arrived

    core = lax.axis_index("slab") % 2
    first = core == 0
    def pick(on_first, on_second):
        return jnp.where(first, on_first, on_second)

    last_chip = lax.axis_index("slab") // 2 == chips - 1
    residual = right_side[0, 0]
    factor = inverse_factor[0, 0]
    columns = residual.shape[0]
    scalars = jnp.stack([core.astype(jnp.int32), margin[0, 0], last_chip.astype(jnp.int32)])
    face = (columns, FACE)
    three, five_, seven = 3 * FACE, 5 * FACE, 7 * FACE

    to_near, to_far, maps = prepare(scalars, residual, factor, forward_trace[0, 0], backward_trace[0, 0])
    near, far = from_near(to_near), from_far(to_far)
    adjusted, near_basis, far_basis, message, outer, extra, up0 = local_operators(
        scalars, residual, near, far, maps
    )

    message_other = swap(message)
    outer_other = swap(outer)
    mine, other = message[columns:], turned(message_other[columns:])
    pack = jnp.concatenate(
        [pick(message[:columns], message_other[:columns]), pick(mine, other), pick(other, mine)], axis=0
    )
    near = from_near(pack)

    def joined(part):
        return (part + swap(part.astype(BF)).astype(F32)).astype(BF)

    nothing = jnp.zeros(face, F32)
    odd_down = pick(turned(outer_other[columns:]), outer[columns:])
    own_down = pick(pack[:columns], jnp.zeros(face, BF))
    base = dot(jnp.concatenate([near[:columns], own_down], axis=1), odd_down[: 2 * FACE])
    base = base + pick(outer_other[:columns].astype(F32), nothing)
    pieces = hop(joined(base), 0, 1, 2)

    far, extra_other = swap(near), swap(extra)
    rows = ((3 * three, FACE), BF)
    band = ((five_, FACE), BF)
    forward, backward, reach, reach_start, even_rows, odd_rows, even_down, turn, even_start = call(
        share_kernel,
        [band, band, ((columns + five_, FACE), BF), (face, F32), rows, rows, ((columns, three), BF),
         ((2 * three, FACE), BF), (face, F32)],
        scalars,
        [near, pack, far, outer, outer_other, extra, extra_other, up0],
        (1 << 10, 1 << 10),
    )

    def step(pieces, base, operator, *later, beside=()):
        pieces, base, operator, later, beside = barrier((pieces, base, operator, later, list(beside)))
        rows = jnp.concatenate([*pieces, *beside], axis=1)
        part = base + dot(rows, operator[: rows.shape[1]])
        part, pieces, beside = barrier((part, pieces, beside))
        return joined(part), jnp.concatenate(pieces[-3:], axis=1), *later, *beside

    def inward(seen):
        return dot(seen, reach[columns : columns + three])

    barrier = lax.optimization_barrier
    total, seen = step(pieces, base, forward)
    pieces = hop(total, 1, 1, 2)
    reach_near = from_near(reach)
    total, new, reach_near, seen = step(pieces, base, forward, reach_near, seen)
    pieces = hop(total, 2, 1, 3)
    seen = seen + new
    reached = inward(seen)

    operator, even_turn = call(
        turn_kernel,
        [((seven, FACE), BF), (face, F32)],
        scalars,
        [reach_near, reach, swap(reach_near), turn, even_start],
        (1 << 10, 1 << 10),
    )
    reached_other = swap(reached)
    total, new, reached_other, operator = step(pieces, even_turn, operator, reached_other, operator)
    pieces = hop(total, 3, -1, 2)

    seen_all = seen + new
    reached_last = inward(new)
    last_other = swap(reached_last)
    reached_other, last_other = barrier((reached_other, last_other))
    own = (reach_start + reached + reached_other).astype(BF)
    near = from_near(own)
    own_part = jnp.concatenate([seen[:, FACE:], pick(own, jnp.zeros(face, BF))], axis=1)
    own_turn = jnp.concatenate([turn[: 2 * FACE], turn[4 * FACE : 5 * FACE]], axis=0)
    near_turn = turn[3 * FACE : 4 * FACE]
    base = pick(even_start, nothing) + dot(own_part, own_turn)
    turned_back = jnp.concatenate([backward[:three], near_turn], axis=0)
    total, seen, last_other, near = step(pieces, base, turned_back, last_other, beside=[near])
    pieces = hop(total, 2, -1, 2)
    base = base + dot(near, near_turn)

    own_last = (reach_start + reached_last + last_other).astype(BF)
    near_last = from_near(own_last)
    seen_other = swap(seen_all)
    down = call(
        faces_kernel, [((columns, three), BF)], scalars, [seen_all, seen_other, even_down, even_rows], (1 << 10, 1 << 10)
    )[0]
    total, new, near_last, down = step(pieces, base, backward, near_last, down)
    pieces = hop(total, 1, -1, 2)
    seen = seen + new
    near, own = jnp.where(last_chip, near_last, near), jnp.where(last_chip, own_last, own)
    settled, operator = call(
        settle_kernel,
        [((columns, M), F32), ((five_, M), BF)],
        scalars,
        [adjusted, near_basis, far_basis, down, near, own, swap(near), odd_rows, factor],
        (1 << 10, 1 << 10),
    )
    pieces, seen, operator = barrier((pieces, seen, operator))
    seen = seen + jnp.concatenate(pieces, axis=1)
    out = settled + dot(barrier(five(seen, swap(seen))), operator)
    return out[None, None]


def solution(mesh):
    placed = (
        P("slab", "patch", None, None),
        P("slab", "patch", None, None),
        P("slab", "patch", None, None),
        P("slab", "patch", None, None),
        P("slab", "patch"),
    )
    return jax.shard_map(
        on_device,
        mesh=mesh,
        in_specs=placed,
        out_specs=P("slab", "patch", None, None),
        check_vma=False,
    )
```
